32 devices in a mesh: shard: 2 (over y), seq: 16 (over z, x, core).
Axes of the slice: x: 2, y: 2, z: 4, core: 2. Of those that a mesh axis runs over, the one named last changes fastest.
Arguments:
- queries: bfloat16 [16384, 1024], P(('shard', 'seq')), parts along dimension 0, may hold values from -112 to 112
- key_rows: bfloat16 [16384, 128], P(('shard', 'seq')), parts along dimension 0, may hold values from -4 to 4
- value_rows: bfloat16 [16384, 128], P(('shard', 'seq')), parts along dimension 0, may hold values from -6 to 6
- out_grads: bfloat16 [16384, 1024], P(('shard', 'seq')), parts along dimension 0, may hold values from -6 to 6
- segment_ids: int32 [16384], P('shard'), parts along dimension 0, may hold values from 0 to 1, never falling along the last dimension, each value on 1 to 7168 neighbouring positions
- random_blocks: int32 [128, 8, 3], P(('shard', 'seq')), parts along dimension 0, may hold values from 0 to 63, as said below
- global_blocks: int32 [4], P('shard'), parts along dimension 0, may hold values from 0 to 63
Outputs:
- attended: bfloat16 [16384, 1024], P(('shard', 'seq')), parts along dimension 0
- d_queries: bfloat16 [16384, 1024], P(('shard', 'seq')), parts along dimension 0
- d_keys: bfloat16 [16384, 128], P(('shard', 'seq')), parts along dimension 0
- d_values: bfloat16 [16384, 128], P(('shard', 'seq')), parts along dimension 0
The draws below stay inside these ranges and needn't reach their ends.
There are 2 independent parts, one for each index of `shard`. The reference program is written for one: setup_inputs(seed, part) draws one part's arguments, and reference() takes and returns one part's arrays. A program takes and returns all parts, laid end to end along the dimension named above; each array names one. Nothing has to cross between parts.
Inputs may be any that keep to these rules, and one draw needn't show every extreme that they name: The 96 names of random_blocks in the rows of one device's 4 query blocks fall on at most 6 of them on any one device along seq, and on exactly 6 for some device.
All inputs are finite; a program needn't handle non-finite values.
Results may differ from the reference program's by a relative error of at most 0.035.
Values may be sent and summed in bfloat16 or wider, within the bound.
A program may use at most 128 MiB of HBM per device.

```python
import math
import jax
import jax.numpy as jnp
import numpy as np
from jax import lax

HD = 128
HQ = 8
BLK = 128
RAND = 3
G = 2
QB_DEV = 4
NB = 64
TOKENS = 8192
N_SEQ = 16


def drawn_pair(key):
    key_draw = jnp.clip(jax.random.normal(jax.random.fold_in(key, 11), (TOKENS, HD), jnp.float32), -4.0, 4.0)
    query_draw = jnp.clip(jax.random.normal(jax.random.fold_in(key, 12), (TOKENS, HQ * HD), jnp.float32), -4.0, 4.0)
    return (query_draw, key_draw)


def draw_queries(key, part):
    return drawn_pair(key)[0].astype(jnp.bfloat16)


def draw_key_rows(key, part):
    return drawn_pair(key)[1].astype(jnp.bfloat16)


def draw_random_blocks(key, part):
    pick_count = QB_DEV * HQ * RAND

    def one_device(device_key):
        owner_order = jax.random.permutation(jax.random.fold_in(device_key, 1), N_SEQ)
        shuffle = jax.random.permutation(jax.random.fold_in(device_key, 2), pick_count)
        owners = owner_order[shuffle % N_SEQ]
        local_ids = jax.random.randint(jax.random.fold_in(device_key, 3), (pick_count,), 0, QB_DEV)
        return (owners * QB_DEV + local_ids).reshape(QB_DEV, HQ, RAND)
    device_keys = jax.random.split(jax.random.fold_in(key, 7), N_SEQ)
    return jax.vmap(one_device)(device_keys).reshape(NB, HQ, RAND).astype(jnp.int32)


def levels(stream_key, dims, cuts, smallest, largest):
    def one(axis_at, parts):
        heights = jax.random.uniform(jax.random.fold_in(jax.random.fold_in(stream_key, 6), axis_at), (parts,), jnp.float32, smallest / len(cuts), largest / len(cuts))
        return jnp.repeat(jnp.exp(heights), dims[axis_at] // parts).reshape((-1,) + (1,) * (len(dims) - axis_at - 1))

    level = one(*cuts[0])
    for cut in cuts[1:]:
        level = level * one(*cut)
    return level


def profile(number_of, total, reach, skew):
    loads = [(1 << 20) // math.isqrt(rank ** skew) + 1 for rank in range(2, number_of + 1)]
    rest, given = total - reach - (number_of - 1), [1] * (number_of - 1)
    while rest > 0:
        candidates = [i for i in range(number_of - 1) if given[i] < reach]
        whole, remaining = sum([loads[i] for i in candidates]), rest
        for i in candidates:
            extra = min(reach - given[i], max(1, remaining * loads[i] // whole), rest)
            given[i] = given[i] + extra
            rest = rest - extra
    return np.array([reach] + given)


def uneven(own_key, number_of, total, reach, lean):
    if number_of == 2:
        one = jax.random.randint(own_key, (), max(1, total - reach), min(reach, total - 1) + 1)
        return jnp.stack([one, total - one])
    lengths = jnp.asarray(profile(number_of, total, reach, lean), jnp.int32)
    twos = (number_of - 1) // 2
    giver, sink = lengths[1:1 + 2 * twos:2], lengths[2:2 + 2 * twos:2]
    slack = jnp.minimum(giver - 1, reach - sink)
    moved = jax.random.randint(jax.random.fold_in(own_key, 1), (twos,), 0, 1 << 20) % (slack + 1)
    lengths = lengths.at[1:1 + 2 * twos:2].set(giver - moved).at[2:2 + 2 * twos:2].set(sink + moved)
    return lengths[jax.random.permutation(jax.random.fold_in(own_key, 2), number_of)]


def scatter_about(stream_key, shape, spread, bound, cuts=(), kind=jnp.bfloat16):
    values = jax.random.normal(stream_key, shape, jnp.float32) * spread
    if len(cuts) > 0:
        values = levels(stream_key, shape, cuts, -0.22, 0.18) * values
    return jnp.clip(values, min=-bound, max=bound).astype(kind)


def setup_inputs(seed: int = 0, part: int = 0) -> dict:
    arg_keys = jax.random.split(jax.random.key(seed), 8)
    part_splits = jax.random.split(jax.random.fold_in(arg_keys[7], part), 8)
    return {
        "queries": draw_queries(jax.random.fold_in(jax.random.fold_in(arg_keys[7], part), 71), part),
        "key_rows": draw_key_rows(jax.random.fold_in(jax.random.fold_in(arg_keys[7], part), 71), part),
        "value_rows": scatter_about(part_splits[2], (TOKENS, HD), 1.0, 6.0, ((0, 16),)),
        "out_grads": scatter_about(part_splits[3], (TOKENS, HQ * HD), 1.0, 6.0, ((0, 16),)),
        "segment_ids": jnp.searchsorted(jnp.cumsum(uneven(part_splits[4], 2, TOKENS, TOKENS - TOKENS // 8, 0)), jnp.arange(TOKENS), side="right").astype(jnp.int32),
        "random_blocks": draw_random_blocks(jax.random.fold_in(jax.random.fold_in(arg_keys[7], part), 71), part),
        "global_blocks": jax.random.randint(part_splits[6], (G,), 0, NB).astype(jnp.int32),
    }


masked_value = -1e+30

def block_pass(query_block, grad_block, shared, shared_live, query_segs, shared_segs, random_kv, random_segs, scaling):
    query_wide = query_block.astype(jnp.float32)
    grad_wide = grad_block.astype(jnp.float32)
    shared_wide = shared.astype(jnp.float32)
    random_wide = random_kv.astype(jnp.float32)
    shared_mask = (query_segs[:, None, None] == shared_segs[None]) & shared_live[None, :, None]
    random_mask = query_segs[None, :, None, None] == random_segs[:, None]
    shared_scores = jnp.einsum('thd,jkd->htjk', query_wide, shared_wide[:, :, :HD]) * scaling
    shared_scores = jnp.where(shared_mask[None], shared_scores, masked_value)
    random_scores = jnp.einsum('thd,hrkd->htrk', query_wide, random_wide[:, :, :, :HD]) * scaling
    random_scores = jnp.where(random_mask, random_scores, masked_value)
    top_score = jnp.maximum(lax.optimization_barrier(jnp.max(shared_scores, axis=(2, 3))), lax.optimization_barrier(jnp.max(random_scores, axis=(2, 3))))
    totals = lax.optimization_barrier(jnp.sum(jnp.exp(shared_scores - top_score[:, :, None, None]), axis=(2, 3)))
    totals = totals + lax.optimization_barrier(jnp.sum(jnp.exp(random_scores - top_score[:, :, None, None]), axis=(2, 3)))
    log_totals = top_score + jnp.log(totals)
    shared_probs = jnp.exp(shared_scores - log_totals[:, :, None, None])
    random_probs = jnp.exp(random_scores - log_totals[:, :, None, None])
    shared_half = shared_probs.astype(jnp.bfloat16).astype(jnp.float32)
    random_half = random_probs.astype(jnp.bfloat16).astype(jnp.float32)
    attended = jnp.einsum('htjk,jkd->thd', shared_half, shared_wide[:, :, HD:])
    attended = (attended + jnp.einsum('htrk,hrkd->thd', random_half, random_wide[:, :, :, HD:])).astype(jnp.bfloat16)
    row_dots = jnp.einsum('thd,thd->ht', grad_wide, attended.astype(jnp.float32))
    shared_dprobs = jnp.einsum('thd,jkd->htjk', grad_wide, shared_wide[:, :, HD:])
    random_dprobs = jnp.einsum('thd,hrkd->htrk', grad_wide, random_wide[:, :, :, HD:])
    shared_dscores = (shared_probs * (shared_dprobs - row_dots[:, :, None, None])).astype(jnp.bfloat16).astype(jnp.float32)
    random_dscores = (random_probs * (random_dprobs - row_dots[:, :, None, None])).astype(jnp.bfloat16).astype(jnp.float32)
    query_grads = jnp.einsum('htjk,jkd->thd', shared_dscores, shared_wide[:, :, :HD])
    query_grads = query_grads + jnp.einsum('htrk,hrkd->thd', random_dscores, random_wide[:, :, :, :HD])
    query_grads = (query_grads * scaling).astype(jnp.bfloat16)
    shared_kgrad = jnp.einsum('htjk,thd->jkd', shared_dscores, query_wide) * scaling
    shared_vgrad = jnp.einsum('htjk,thd->jkd', shared_half, grad_wide)
    shared_grads = jnp.where(shared_live[:, None, None], jnp.concatenate([shared_kgrad, shared_vgrad], axis=2), 0.0)
    random_kgrad = jnp.einsum('htrk,thd->hrkd', random_dscores, query_wide) * scaling
    random_vgrad = jnp.einsum('htrk,thd->hrkd', random_half, grad_wide)
    random_grads = jnp.concatenate([random_kgrad, random_vgrad], axis=3)
    return (attended, query_grads, shared_grads, random_grads)

def reference(queries, key_rows, value_rows, out_grads, segment_ids, random_blocks, global_blocks):
    scaling = 1.0 / math.sqrt(HD)
    joined = jnp.concatenate([key_rows, value_rows], axis=1).reshape(NB, BLK, 2 * HD)
    seg_blocks = segment_ids.reshape(NB, BLK)
    query_blocks = queries.reshape(NB, BLK, HQ, HD)
    grad_blocks = out_grads.reshape(NB, BLK, HQ, HD)
    global_ids = global_blocks.astype(jnp.int32)

    def advance(gradients, block_index):
        window_ids = block_index + jnp.arange(-1, 2, dtype=jnp.int32)
        window_live = (window_ids >= 0) & (window_ids < NB)
        shared_ids = jnp.concatenate([jnp.clip(window_ids, 0, NB - 1), global_ids])
        shared_live = jnp.concatenate([window_live, jnp.ones((G,), bool)])
        random_ids = random_blocks[block_index].astype(jnp.int32)
        attended, query_grads, shared_grads, random_grads = block_pass(query_blocks[block_index], grad_blocks[block_index], joined[shared_ids], shared_live, seg_blocks[block_index], seg_blocks[shared_ids], joined[random_ids], seg_blocks[random_ids], scaling)
        gradients = gradients.at[shared_ids].add(shared_grads)
        gradients = gradients.at[random_ids.reshape(-1)].add(random_grads.reshape(HQ * RAND, BLK, 2 * HD))
        return (gradients, (attended, query_grads))
    start_grads = jnp.zeros((NB, BLK, 2 * HD), jnp.float32)
    gradients, (attended, query_grads) = lax.scan(advance, start_grads, jnp.arange(NB, dtype=jnp.int32))
    flat_grads = gradients.reshape(TOKENS, 2 * HD)
    return (attended.reshape(TOKENS, HQ * HD), query_grads.reshape(TOKENS, HQ * HD), flat_grads[:, :HD].astype(jnp.bfloat16), flat_grads[:, HD:].astype(jnp.bfloat16))
```

```python
import math

import jax
import jax.numpy as jnp
from jax import lax
from jax.experimental import pallas as pl
from jax.experimental.pallas import tpu as pltpu
from jax.sharding import PartitionSpec as P

HD = 128
HQ = 8
BLK = 128
RAND = 3
G = 2


masked_value = -1e30


def with_halo(array, sides, width):
    for axis, dim in sides:
        size, length = (lax.axis_size(axis), array.shape[dim])
        up = [(i, (i + 1) % size) for i in range(size - 1)]
        down = [(j, i) for i, j in up]
        last = lax.slice_in_dim(array, length - width, length, axis=dim)
        first = lax.slice_in_dim(array, 0, width, axis=dim)
        before = lax.ppermute(last, axis, up)
        after = lax.ppermute(first, axis, down)
        array = jnp.concatenate([before, array, after], axis=dim)
    return array


def spread(block, axis, owner):
    block = jnp.where(lax.axis_index(axis) == owner, block, jnp.zeros_like(block))
    return lax.psum(block, axis)


def from_behind(block, axis, distance):
    devices = range(lax.axis_size(axis))
    route = [(i - distance, i) for i in devices if i - distance in devices]
    return lax.ppermute(block, axis, route)


def routing(block_ids, per_device):
    owners = block_ids // per_device
    ordering = jnp.arange(block_ids.shape[0])
    earlier = (owners[:, None] == owners[None, :]) & (ordering[None, :] < ordering[:, None])
    return (owners, jnp.sum(earlier.astype(jnp.int32), axis=1))


def taken(blocks, indices):
    return lax.map(lambda i: lax.dynamic_index_in_dim(blocks, i, 0, keepdims=False), indices)


def block_pass(
    query_block,
    grad_block,
    shared,
    shared_live,
    query_segs,
    shared_segs,
    random_kv,
    random_segs,
    scaling,
):
    wide = jnp.float32
    shared_mask = (query_segs[:, None, None] == shared_segs[None]) & shared_live[None, :, None]
    random_mask = query_segs[None, :, None, None] == random_segs[:, None]
    shared_scores = (
        jnp.einsum("thd,jkd->htjk", query_block, shared[:, :, :HD], preferred_element_type=wide)
        * scaling
    )
    shared_scores = jnp.where(shared_mask[None], shared_scores, masked_value)
    random_scores = (
        jnp.einsum(
            "thd,hrkd->htrk", query_block, random_kv[:, :, :, :HD], preferred_element_type=wide
        )
        * scaling
    )
    random_scores = jnp.where(random_mask, random_scores, masked_value)
    top_score = jnp.maximum(
        jnp.max(shared_scores, axis=(2, 3)), jnp.max(random_scores, axis=(2, 3))
    )
    totals = jnp.sum(jnp.exp(shared_scores - top_score[:, :, None, None]), axis=(2, 3))
    totals = totals + jnp.sum(jnp.exp(random_scores - top_score[:, :, None, None]), axis=(2, 3))
    log_totals = top_score + jnp.log(totals)
    shared_probs = jnp.exp(shared_scores - log_totals[:, :, None, None])
    random_probs = jnp.exp(random_scores - log_totals[:, :, None, None])
    shared_half = shared_probs.astype(jnp.bfloat16)
    random_half = random_probs.astype(jnp.bfloat16)
    attended = jnp.einsum(
        "htjk,jkd->thd", shared_half, shared[:, :, HD:], preferred_element_type=wide
    )
    attended = attended + jnp.einsum(
        "htrk,hrkd->thd", random_half, random_kv[:, :, :, HD:], preferred_element_type=wide
    )
    attended = attended.astype(jnp.bfloat16)
    row_dots = jnp.einsum("thd,thd->ht", grad_block, attended, preferred_element_type=wide)
    shared_dprobs = jnp.einsum(
        "thd,jkd->htjk", grad_block, shared[:, :, HD:], preferred_element_type=wide
    )
    random_dprobs = jnp.einsum(
        "thd,hrkd->htrk", grad_block, random_kv[:, :, :, HD:], preferred_element_type=wide
    )
    shared_dscores = (shared_probs * (shared_dprobs - row_dots[:, :, None, None])).astype(
        jnp.bfloat16
    )
    random_dscores = (random_probs * (random_dprobs - row_dots[:, :, None, None])).astype(
        jnp.bfloat16
    )
    query_grads = jnp.einsum(
        "htjk,jkd->thd", shared_dscores, shared[:, :, :HD], preferred_element_type=wide
    )
    query_grads = query_grads + jnp.einsum(
        "htrk,hrkd->thd", random_dscores, random_kv[:, :, :, :HD], preferred_element_type=wide
    )
    query_grads = (query_grads * scaling).astype(jnp.bfloat16)
    shared_kgrad = (
        jnp.einsum("htjk,thd->jkd", shared_dscores, query_block, preferred_element_type=wide)
        * scaling
    )
    shared_vgrad = jnp.einsum("htjk,thd->jkd", shared_half, grad_block, preferred_element_type=wide)
    shared_grads = jnp.where(
        shared_live[:, None, None], jnp.concatenate([shared_kgrad, shared_vgrad], axis=2), 0.0
    )
    random_kgrad = (
        jnp.einsum("htrk,thd->hrkd", random_dscores, query_block, preferred_element_type=wide)
        * scaling
    )
    random_vgrad = jnp.einsum(
        "htrk,thd->hrkd", random_half, grad_block, preferred_element_type=wide
    )
    random_grads = jnp.concatenate([random_kgrad, random_vgrad], axis=3)
    return (attended, query_grads, shared_grads, random_grads, log_totals, row_dots)


def body(queries, key_rows, value_rows, out_grads, segment_ids, random_blocks, global_blocks):
    scaling = 1.0 / math.sqrt(HD)
    row_count = queries.shape[0]
    qcount = row_count // BLK
    devices = lax.axis_size("seq")
    position = lax.axis_index("seq")
    total_blocks = segment_ids.shape[0] // BLK
    seg_blocks = segment_ids.reshape(total_blocks, BLK)
    joined = jnp.concatenate([key_rows, value_rows], axis=1)
    local_blocks = joined.reshape(qcount, BLK, 2 * HD)
    padded = with_halo(joined, (("seq", 0),), BLK)
    owned = global_blocks // qcount == position
    pieces = []
    for global_slot in range(G):
        picked = lax.dynamic_index_in_dim(
            local_blocks, global_blocks[global_slot] % qcount, 0, keepdims=False
        )
        pieces.append(spread(picked, "seq", global_blocks[global_slot] // qcount))
    global_kv = jnp.stack(pieces)
    chosen_ids = random_blocks.reshape(-1)
    pick_count = chosen_ids.shape[0]
    capacity = -(-pick_count // devices)
    owners, slots = routing(chosen_ids, qcount)
    outgoing_ids = (
        jnp.full((devices, capacity), -1, jnp.int32).at[owners, slots].set(chosen_ids % qcount)
    )
    wanted = lax.all_to_all(outgoing_ids, "seq", split_axis=0, concat_axis=0, tiled=True)
    wanted_clip = jnp.clip(wanted, 0, qcount - 1)
    served = taken(local_blocks, wanted_clip.reshape(-1)).reshape(wanted.shape + (BLK, 2 * HD))
    answer = lax.all_to_all(served, "seq", split_axis=0, concat_axis=0, tiled=True)
    answer = answer.reshape(devices * capacity, BLK, 2 * HD)
    random_kv = taken(answer, owners * capacity + slots)
    random_kv = random_kv.reshape(qcount, HQ, RAND, BLK, 2 * HD)
    query_blocks = queries.reshape(qcount, BLK, HQ, HD)
    grad_blocks = out_grads.reshape(qcount, BLK, HQ, HD)

    def attend(bundle):
        block_index, query_block, grad_block, block_kv, block_ids = bundle
        global_index = position * qcount + block_index
        window = lax.dynamic_slice_in_dim(padded, block_index * BLK, 3 * BLK, 0).reshape(
            3, BLK, 2 * HD
        )
        window_ids = global_index + jnp.arange(-1, 2, dtype=jnp.int32)
        window_live = (window_ids >= 0) & (window_ids < total_blocks)
        shared_ids = jnp.concatenate([jnp.clip(window_ids, 0, total_blocks - 1), global_blocks])
        shared_live = jnp.concatenate([window_live, jnp.ones((G,), bool)])
        shared = jnp.concatenate([window, global_kv], axis=0)
        return block_pass(
            query_block,
            grad_block,
            shared,
            shared_live,
            seg_blocks[global_index],
            seg_blocks[shared_ids],
            block_kv,
            seg_blocks[block_ids],
            scaling,
        )

    attended, query_grads, shared_grads, random_grads, log_totals, row_dots = lax.map(
        attend,
        (jnp.arange(qcount, dtype=jnp.int32), query_blocks, grad_blocks, random_kv, random_blocks),
    )
    window_sum = jnp.zeros((qcount + 2, BLK, 2 * HD), jnp.float32)
    for offset in range(3):
        window_sum = window_sum.at[offset : offset + qcount].add(shared_grads[:, offset])
    from_right = from_behind(window_sum[0].astype(jnp.bfloat16), "seq", -1).astype(jnp.float32)
    from_left = from_behind(window_sum[qcount + 1].astype(jnp.bfloat16), "seq", 1).astype(
        jnp.float32
    )
    own_grads = window_sum[1 : qcount + 1]
    own_grads = own_grads.at[qcount - 1].add(from_right).at[0].add(from_left)
    global_sum = lax.psum(jnp.sum(shared_grads[:, 3:], axis=0), "seq")
    global_hits = (
        (global_blocks[:, None] % qcount == jnp.arange(qcount)[None, :]) & owned[:, None]
    ).astype(jnp.float32)
    own_grads = own_grads + jnp.einsum(
        "gq,gkd->qkd", global_hits, global_sum, precision=lax.Precision.HIGHEST
    )
    outgoing = (
        jnp.zeros((devices, capacity, BLK, 2 * HD), jnp.float32)
        .at[owners, slots]
        .set(random_grads.reshape(pick_count, BLK, 2 * HD))
    )
    returned = lax.all_to_all(outgoing, "seq", split_axis=0, concat_axis=0, tiled=True)
    request_hits = (wanted[:, :, None] == jnp.arange(qcount)[None, None, :]).astype(jnp.float32)
    own_grads = own_grads + jnp.einsum(
        "ncq,nckd->qkd", request_hits, returned, precision=lax.Precision.HIGHEST
    )
    own_flat = own_grads.reshape(row_count, 2 * HD)
    return (
        attended.reshape(row_count, HQ * HD),
        query_grads.reshape(row_count, HQ * HD),
        own_flat[:, :HD].astype(jnp.bfloat16),
        own_flat[:, HD:].astype(jnp.bfloat16),
    )


LOG2E = 1.4426950408889634
DENSE_BYTES = 16 * 1024 * 1024
LINE = 4
SEQ = 16


class Place:
    def __init__(self):
        me = lax.axis_index("seq")
        self.me = me
        self.core = lax.rem(me, 2)
        self.x = lax.rem(me // 2, 2)
        self.z = me // 4
        self.high = self.z // 2
        self.step = 1 - 2 * self.high
        self.inner = jnp.where((self.z == 1) | (self.z == 2), 1, 0)
        self.partner = self.at(self.z, self.x, 1 - self.core)
        self.across = self.at(self.z, 1 - self.x, self.core)
        self.onward = self.at(self.z + self.step, self.x, self.core)
        self.outward = self.at(self.z - self.step, self.x, self.core)

    def at(self, z, x, core):
        return z * 4 + x * 2 + core


def greet(place):
    barrier = pltpu.get_barrier_semaphore()
    for other in (place.partner, place.across, place.onward):
        pl.semaphore_signal(
            barrier, inc=1, device_id={"seq": other}, device_id_type=pl.DeviceIdType.MESH
        )

    @pl.when(place.inner == 1)
    def _():
        pl.semaphore_signal(
            barrier, inc=1, device_id={"seq": place.outward}, device_id_type=pl.DeviceIdType.MESH
        )

    pl.semaphore_wait(barrier, 3 + place.inner)


def remote(source, target, send, receive, device):
    return pltpu.make_async_remote_copy(
        src_ref=source,
        dst_ref=target,
        send_sem=send,
        recv_sem=receive,
        device_id={"seq": device},
        device_id_type=pl.DeviceIdType.MESH,
    )


ROWS = 4
PICKS = ROWS * HQ * RAND
EACH = PICKS // SEQ
HALVES = 2


class Gather:
    def __init__(self, place, buffer, zs, zr, xs, xr, cs, cr):
        self.place = place
        z, step, inner = place.z, place.step, place.inner
        lines = [z, z + step - 2 * step * inner, z + step * (2 - inner), z + step * (3 - inner)]
        self.own = [place.at(line, place.x, place.core) for line in lines]
        self.other = [place.at(line, 1 - place.x, place.core) for line in lines]
        self.own_far = [place.at(line, place.x, 1 - place.core) for line in lines]
        self.other_far = [place.at(line, 1 - place.x, 1 - place.core) for line in lines]
        width = ROWS // HALVES

        def copies(owner, sends, at, receives, to, device):
            made = []
            for half in range(HALVES):
                part = buffer.at[pl.ds(owner * ROWS + half * width, width)]
                made.append(
                    remote(
                        part,
                        part,
                        sends.at[at * HALVES + half],
                        receives.at[to * HALVES + half],
                        device,
                    )
                )
            return made

        onward, outward = place.onward, place.outward
        own, other = self.own, self.other
        self.edge = copies(own[0], zs, 0, zr, 1, onward)
        self.along = copies(own[0], zs, 0, zr, 2, onward)
        self.out = copies(own[0], zs, 1, zr, 1, outward)
        self.relays = [
            copies(own[1], zs, 2, zr, 3, onward),
            copies(own[2], zs, 3, zr, 2, outward),
            copies(own[3], zs, 4, zr, 3, outward),
        ]
        self.arrivals = [copies(own[k], zs, 0, zr, k, onward) for k in range(LINE)]
        self.crossing = [copies(own[k], xs, k, xr, k, place.across) for k in range(LINE)]
        self.crossed = [copies(other[k], xs, k, xr, k, place.across) for k in range(LINE)]
        self.near = [copies(own[k], cs, k, cr, k, place.partner) for k in range(LINE)]
        self.far = [copies(other[k], cs, LINE + k, cr, LINE + k, place.partner) for k in range(LINE)]

    def start_line(self):
        @pl.when(self.place.inner == 0)
        def _():
            for copy in self.edge:
                copy.start()

        @pl.when(self.place.inner == 1)
        def _():
            for half in range(HALVES):
                self.out[half].start()
                self.along[half].start()

    def start_cross(self):
        for half in range(HALVES):
            self.crossing[0][half].start()
            self.near[0][half].start()

    def line_arrival(self, k):
        for half in range(HALVES):
            self.arrivals[k][half].wait_recv()

            @pl.when(self.place.inner == 1)
            def _(half=half):
                self.relays[k - 1][half].start()

            self.crossing[k][half].start()
            self.near[k][half].start()

    def cross_arrival(self, k):
        for half in range(HALVES):
            self.crossed[k][half].wait_recv()
            self.far[k][half].start()

    def near_arrival(self, k):
        for half in range(HALVES):
            self.near[k][half].wait_recv()

    def far_arrival(self, k):
        for half in range(HALVES):
            self.far[k][half].wait_recv()

    def wait_sends(self):
        for half in range(HALVES):
            self.edge[half].wait_send()
            for k in range(LINE):
                self.crossing[k][half].wait_send()
                self.near[k][half].wait_send()
                self.far[k][half].wait_send()

        @pl.when(self.place.inner == 1)
        def _():
            for half in range(HALVES):
                self.out[half].wait_send()
                for relay in self.relays:
                    relay[half].wait_send()


class Scatter:
    def __init__(
        self, place, kept, pair_out, pair_in, cross_out, cross_in, line_out, line_in,
        ps, pr, xs, xr, zs, zr,
    ):
        self.place = place
        self.kept, self.pair_out, self.pair_in = kept, pair_out, pair_in
        self.cross_out, self.cross_in = cross_out, cross_in
        self.line_out, self.line_in = line_out, line_in
        self.sems = (ps, pr, xs, xr, zs, zr)
        z, high = place.z, place.high
        self.order = [3 * (1 - high), 2 - high, 1 - z + 4 * high, z]

    def pair(self, index):
        ps, pr = self.sems[:2]
        return remote(
            self.pair_out.at[index], self.pair_in.at[index], ps.at[index], pr.at[index],
            self.place.partner,
        )

    def cross(self, k):
        xs, xr = self.sems[2:4]
        return remote(
            self.cross_out.at[k], self.cross_in.at[k], xs.at[k], xr.at[k], self.place.across
        )

    def hop(self, k, slot, device):
        zs, zr = self.sems[4:]
        return remote(self.line_out.at[k], self.line_in.at[slot], zs.at[k], zr.at[slot], device)

    def start_cross(self, k):
        self.pair(2 * k).wait_recv()
        total = self.kept[2 * k] + self.pair_in[2 * k].astype(jnp.float32)
        self.cross_out[k] = total.astype(jnp.bfloat16)
        self.cross(k).start()

    def local(self, k):
        wide = jnp.float32
        return self.kept[2 * k + 1] + self.pair_in[2 * k + 1].astype(wide) + self.cross_in[k].astype(wide)

    def arrived(self, slot):
        self.hop(0, slot, self.place.onward).wait_recv()
        return self.line_in[slot].astype(jnp.float32)

    def start_hop(self, k):
        place = self.place
        self.pair(2 * k + 1).wait_recv()
        self.cross(k).wait_recv()

        @pl.when(place.inner == 0)
        def _():
            self.line_out[k] = self.local(k).astype(jnp.bfloat16)
            self.hop(k, k, place.onward).start()

        @pl.when(place.inner == 1)
        def _():
            total = self.local(k) + self.arrived(k if k < 2 else 3)
            self.line_out[k] = total.astype(jnp.bfloat16)
            if k < 2:
                self.hop(k, 3 + k, place.onward).start()
            else:
                self.hop(k, 0, place.outward).start()

    def finish(self, result):
        k = LINE - 1
        self.pair(2 * k + 1).wait_recv()
        self.cross(k).wait_recv()

        @pl.when(self.place.inner == 0)
        def _():
            result[...] = (self.local(k) + self.arrived(0)).astype(result.dtype)

        @pl.when(self.place.inner == 1)
        def _():
            result[...] = (self.local(k) + self.arrived(2) + self.arrived(4)).astype(result.dtype)

    def wait_sends(self):
        for index in range(2 * LINE):
            self.pair(index).wait_send()
        for k in range(LINE):
            self.cross(k).wait_send()
        for k in range(LINE - 1):
            self.hop(k, k, self.place.onward).wait_send()


def pick_table(random_ref, table_ref):
    shape = (BLK, BLK)
    lane = lax.broadcasted_iota(jnp.int32, shape, 1)
    row = lax.broadcasted_iota(jnp.int32, shape, 0)
    far = 1 << 20
    by_lane = jnp.full((8, BLK), far, jnp.int32)
    small = lax.broadcasted_iota(jnp.int32, (8, BLK), 1)
    by_row = jnp.full(shape, far, jnp.int32)
    for pick in range(PICKS):
        name = random_ref[pick % RAND, pick // (HQ * RAND), pick // RAND % HQ]
        by_lane = jnp.where(small == pick, name * BLK, by_lane)
        by_row = jnp.where(row == pick, name * BLK, by_row)
    by_lane = by_lane + small
    by_row = by_row + row
    rank = jnp.sum((by_lane[0:1] < by_row).astype(jnp.int32), axis=1, keepdims=True)
    code = row * 64 + ((row * 171) >> 9)
    ordered = jnp.sum(jnp.where(rank == lane, code, 0), axis=0, keepdims=True)
    before = jnp.sum((by_row < lane * BLK).astype(jnp.int32), axis=0, keepdims=True)
    table_ref[0:1] = ordered
    table_ref[1:2] = before


def against(rows, columns):
    return lax.dot_general(
        rows, columns, (((1,), (1,)), ((), ())), preferred_element_type=jnp.float32
    )


def product(rows, columns):
    return jnp.dot(rows, columns, preferred_element_type=jnp.float32)


def entries(source, shared_ids, random_ids, parts):
    stack = jnp.concatenate(parts, axis=0)
    tiles = [against(source[i], stack) for i in shared_ids]
    for names in random_ids:
        tiles.append(
            jnp.concatenate([against(source[i], part) for i, part in zip(names, parts)], axis=1)
        )
    return tiles


def gathered(turned, shared_ids, random_ids, tiles):
    shared = product(
        jnp.concatenate([turned[i] for i in shared_ids], axis=1),
        jnp.concatenate(tiles[:5], axis=0),
    )
    pieces = []
    for head in range(HQ):
        names = [random_ids[pick][head] for pick in range(RAND)]
        pieces.append(
            product(
                jnp.concatenate([turned[i] for i in names], axis=1),
                jnp.concatenate(
                    [tile[:, head * BLK : (head + 1) * BLK] for tile in tiles[5:]], axis=0
                ),
            )
        )
    return shared + jnp.concatenate(pieces, axis=1)


def names_of(mine, block, random_ref, global_ref, total_blocks):
    shared_ids = [
        jnp.maximum(mine - 1, 0),
        mine,
        jnp.minimum(mine + 1, total_blocks - 1),
        global_ref[0],
        global_ref[1],
    ]
    random_ids = [[random_ref[pick, block, head] for head in range(HQ)] for pick in range(RAND)]
    return shared_ids, random_ids


def add_shared(block, tiles, stack, window_ref, global_sum_ref):
    for slot in range(3):
        window_ref[block + slot] += product(tiles[slot], stack)
    for slot in range(G):
        global_sum_ref[slot] += product(tiles[3 + slot], stack)


def score_block(
    block, mine, boundary, random_ref, global_ref, query_ref, grad_ref, key_ref,
    shared_ref, picked_ref, window_ref, global_sum_ref,
):
    wide = jnp.float32
    total_blocks = key_ref.shape[0]
    shared_ids, random_ids = names_of(mine, block, random_ref, global_ref, total_blocks)
    dead = [
        jnp.where(mine == 0, masked_value, 0.0).astype(wide),
        None,
        jnp.where(mine == total_blocks - 1, masked_value, 0.0).astype(wide),
        None,
        None,
    ]
    queries = [query_ref[block, head] for head in range(HQ)]
    grads = [grad_ref[block, head] for head in range(HQ)]
    key_row = lax.broadcasted_iota(jnp.int32, (BLK, HD), 0)
    query_low = lax.broadcasted_iota(jnp.int32, (BLK, HD), 1) < boundary - mine * BLK

    def allowed(name):
        return (key_row < boundary - name * BLK) == query_low

    scores = entries(key_ref, shared_ids, random_ids, queries)
    factor = LOG2E / math.sqrt(HD)
    masked = []
    for slot, tile in enumerate(scores):
        pieces = []
        for head in range(HQ):
            piece = tile[:, head * BLK : (head + 1) * BLK] * factor
            name = shared_ids[slot] if slot < 5 else random_ids[slot - 5][head]
            piece = jnp.where(allowed(name), piece, masked_value)
            if slot < 5 and dead[slot] is not None:
                piece = piece + dead[slot]
            pieces.append(piece)
        masked.append(jnp.concatenate(pieces, axis=1))
    top = masked[0]
    for tile in masked[1:]:
        top = jnp.maximum(top, tile)
    top = jnp.max(top, axis=0, keepdims=True)
    powers = [jnp.exp2(tile - top) for tile in masked]
    total = powers[0]
    for tile in powers[1:]:
        total = total + tile
    inverse = 1.0 / jnp.sum(total, axis=0, keepdims=True)
    probs = [(tile * inverse).astype(jnp.bfloat16) for tile in powers]
    for slot in range(5):
        shared_ref[block, slot] = probs[slot]
    for pick in range(RAND):
        for head in range(HQ):
            picked_ref[(block * HQ + head) * RAND + pick] = probs[5 + pick][
                :, head * BLK : (head + 1) * BLK
            ]
    add_shared(block, probs, jnp.concatenate(grads, axis=0), window_ref, global_sum_ref)


def grad_block(
    block, mine, random_ref, global_ref, query_ref, grad_ref, value_ref, key_turned, value_turned,
    shared_ref, picked_ref, dpicked_ref, window_ref, global_sum_ref, attended_ref, query_grad_ref,
):
    wide = jnp.float32
    half = jnp.bfloat16
    total_blocks = value_ref.shape[0]
    shared_ids, random_ids = names_of(mine, block, random_ref, global_ref, total_blocks)
    queries = [query_ref[block, head] for head in range(HQ)]
    grads = [grad_ref[block, head] for head in range(HQ)]
    probs = [shared_ref[block, slot] for slot in range(5)]
    for pick in range(RAND):
        probs.append(
            jnp.concatenate(
                [picked_ref[(block * HQ + head) * RAND + pick] for head in range(HQ)], axis=1
            )
        )
    rows = pl.ds(pl.multiple_of(block * BLK, BLK), BLK)
    attended = gathered(value_turned, shared_ids, random_ids, probs).astype(half).astype(wide)
    grads_turned = jnp.concatenate([part.astype(wide).T for part in grads], axis=1)
    row_dots = jnp.sum(attended * grads_turned, axis=0, keepdims=True)
    for head in range(HQ):
        span = slice(head * BLK, (head + 1) * BLK)
        attended_ref[rows, span] = attended[:, span].T.astype(half)
    dprobs = entries(value_ref, shared_ids, random_ids, grads)
    dscores = [(p.astype(wide) * (d - row_dots)).astype(half) for p, d in zip(probs, dprobs)]
    for pick in range(RAND):
        for head in range(HQ):
            dpicked_ref[(block * HQ + head) * RAND + pick] = dscores[5 + pick][
                :, head * BLK : (head + 1) * BLK
            ]
    add_shared(block, dscores, jnp.concatenate(queries, axis=0), window_ref, global_sum_ref)
    query_grads = gathered(key_turned, shared_ids, random_ids, dscores) / math.sqrt(HD)
    for head in range(HQ):
        span = slice(head * BLK, (head + 1) * BLK)
        query_grad_ref[rows, span] = query_grads[:, span].T.astype(half)


def sum_owner(
    index, scatter, scale, table, global_ref, tiles_ref, rows_ref, window_ref, global_sum_ref,
    running_ref, owner_ref,
):
    place = scatter.place
    k, turn = index // 4, lax.rem(index, 4)
    side, kind = lax.rem(turn, 2), turn // 2
    line = scatter.order[3]
    for other in (2, 1, 0):
        line = jnp.where(k == other, scatter.order[other], line)
    x = jnp.where(side == 0, 1 - place.x, place.x)
    core = jnp.where(kind == 0, 1 - place.core, place.core)
    owner = place.at(line, x, core)
    running = None
    for pick in range(EACH):
        code = table[0, owner * EACH + pick]
        term = product(tiles_ref[code >> 6], rows_ref[(code >> 3) & 7, code & 7])
        running = term if running is None else running + term
        running_ref[pick + 1] = running
    for row in range(ROWS):
        name = owner * ROWS + row
        first = jnp.clip(table[1, name] - owner * EACH, 0, EACH)
        last = jnp.clip(table[1, name + 1] - owner * EACH, 0, EACH)
        total = running_ref[last] - running_ref[first]
        for slot in range(G):
            total = total + global_sum_ref[slot] * jnp.where(global_ref[slot] == name, 1.0, 0.0)
        owner_ref[row] = total

    @pl.when(owner == place.me)
    def _():
        for row in range(ROWS):
            owner_ref[row] += window_ref[1 + row]

    @pl.when(owner == place.me - 1)
    def _():
        owner_ref[ROWS - 1] += window_ref[0]

    @pl.when(owner == place.me + 1)
    def _():
        owner_ref[0] += window_ref[ROWS + 1]

    slot = 2 * k + side

    @pl.when(kind == 0)
    def _():
        scatter.pair_out[slot] = (owner_ref[...] * scale).astype(jnp.bfloat16)
        scatter.pair(slot).start()

    @pl.when(kind == 1)
    def _():
        scatter.kept[slot] = owner_ref[...] * scale


def fused_kernel(
    random_ref, global_ref, segment_ref, query_in, grad_in, key_in, value_in,
    attended_ref, query_grad_ref, key_grad_ref, value_grad_ref,
    keys, values, key_turned, value_turned, queries, grads, shared_ref, picked_ref, dpicked_ref,
    window_ref, global_sum_ref, running_ref, owner_ref, table_vec, table, local_sems,
    *rest,
):
    place = Place()
    wide = jnp.float32
    total_blocks = keys.shape[0]
    key_sems, value_sems, rest = rest[:6], rest[6:12], rest[12:]
    value_scatter = Scatter(place, *rest[:13])
    key_scatter = Scatter(place, *rest[13:])
    me = place.me
    first = me * ROWS
    own = pl.ds(first, ROWS)
    loads = [
        pltpu.make_async_copy(key_in, keys.at[own], local_sems.at[0]),
        pltpu.make_async_copy(value_in, values.at[own], local_sems.at[1]),
    ]
    for head in range(HQ):
        span = pl.ds(head * HD, HD)
        loads.append(
            pltpu.make_async_copy(
                query_in.at[:, :, span], queries.at[:, head], local_sems.at[2 + head]
            )
        )
        loads.append(
            pltpu.make_async_copy(
                grad_in.at[:, :, span], grads.at[:, head], local_sems.at[2 + HQ + head]
            )
        )
    for load in loads:
        load.start()
    greet(place)
    for load in loads[:2]:
        load.wait()
    key_gather = Gather(place, keys, *key_sems)
    value_gather = Gather(place, values, *value_sems)

    def turn(source, target, owner):
        for row in range(ROWS):
            target[owner * ROWS + row] = source[owner * ROWS + row].T

    def turn_keys(owner):
        turn(keys, key_turned, owner)

    def turn_values(owner):
        turn(values, value_turned, owner)

    key_gather.start_line()
    key_gather.start_cross()
    value_gather.start_cross()
    pick_table(random_ref, table_vec)
    table_copy = pltpu.make_async_copy(table_vec, table, local_sems.at[2 + 2 * HQ])
    table_copy.start()
    zero = jnp.zeros((BLK, HD), wide)

    def clear():
        for row in range(ROWS + 2):
            window_ref[row] = zero
        for slot in range(G):
            global_sum_ref[slot] = zero

    clear()
    running_ref[0] = zero
    boundary = jnp.sum((segment_ref[...] == segment_ref[0:1, 0:1]).astype(jnp.int32))
    for k in range(1, LINE):
        key_gather.line_arrival(k)
        key_gather.cross_arrival(k - 1)
        if k == 1:
            value_gather.start_line()
        turn_keys(key_gather.own[k - 1])
        turn_keys(key_gather.other[k - 1])
        if k > 1:
            key_gather.near_arrival(k - 2)
            turn_keys(key_gather.own_far[k - 2])
            key_gather.far_arrival(k - 2)
            turn_keys(key_gather.other_far[k - 2])
    value_gather.line_arrival(1)
    value_gather.cross_arrival(0)
    turn_keys(key_gather.own[LINE - 1])
    key_gather.near_arrival(LINE - 2)
    turn_keys(key_gather.own_far[LINE - 2])
    key_gather.far_arrival(LINE - 2)
    turn_keys(key_gather.other_far[LINE - 2])
    key_gather.cross_arrival(LINE - 1)
    key_gather.near_arrival(LINE - 1)
    turn_keys(key_gather.own_far[LINE - 1])
    turn_keys(key_gather.other[LINE - 1])
    key_gather.far_arrival(LINE - 1)
    turn_keys(key_gather.other_far[LINE - 1])
    for load in loads[2:]:
        load.wait()
    table_copy.wait()

    @pl.loop(0, ROWS)
    def _(block):
        score_block(
            block, first + block, boundary, random_ref, global_ref, queries, grads, keys,
            shared_ref, picked_ref, window_ref, global_sum_ref,
        )

        @pl.when(block == 0)
        def _():
            value_gather.line_arrival(2)
            value_gather.cross_arrival(1)

        @pl.when(block == 1)
        def _():
            value_gather.line_arrival(3)
            value_gather.cross_arrival(2)

        @pl.when(block == 2)
        def _():
            value_gather.cross_arrival(3)

    @pl.loop(0, SEQ)
    def _(index):
        sum_owner(
            index, value_scatter, 1.0, table, global_ref, picked_ref, grads, window_ref,
            global_sum_ref, running_ref, owner_ref,
        )
        for k in range(LINE):

            @pl.when(index == 4 * k + 3)
            def _(k=k):
                value_scatter.start_cross(k)

    clear()
    for k in range(LINE):
        turn_values(value_gather.own[k])
        turn_values(value_gather.other[k])
        value_gather.near_arrival(k)
        turn_values(value_gather.own_far[k])
        value_gather.far_arrival(k)
        turn_values(value_gather.other_far[k])

    @pl.loop(0, ROWS)
    def _(block):
        grad_block(
            block, first + block, random_ref, global_ref, queries, grads, values, key_turned,
            value_turned, shared_ref, picked_ref, dpicked_ref, window_ref, global_sum_ref,
            attended_ref, query_grad_ref,
        )
        for k in range(LINE - 1):

            @pl.when(block == k)
            def _(k=k):
                value_scatter.start_hop(k)

    @pl.loop(0, SEQ)
    def _(index):
        sum_owner(
            index, key_scatter, 1.0 / math.sqrt(HD), table, global_ref, dpicked_ref, queries,
            window_ref, global_sum_ref, running_ref, owner_ref,
        )
        for k in range(LINE):

            @pl.when(index == 4 * k + 3)
            def _(k=k):
                key_scatter.start_cross(k)

    value_scatter.finish(value_grad_ref)
    for k in range(LINE - 1):
        key_scatter.start_hop(k)
    key_scatter.finish(key_grad_ref)
    key_gather.wait_sends()
    value_gather.wait_sends()
    value_scatter.wait_sends()
    key_scatter.wait_sends()


def fused_call(random_ids, global_ids, segments, queries, out_grads, keys, values):
    vmem = pl.BlockSpec(memory_space=pltpu.VMEM)
    smem = pl.BlockSpec(memory_space=pltpu.SMEM)
    hbm = pl.BlockSpec(memory_space=pl.ANY)
    half = jnp.bfloat16
    wide = jnp.float32
    total_blocks = SEQ * ROWS
    dma = pltpu.SemaphoreType.DMA

    def tiles(*count, kind=half):
        return pltpu.VMEM(count + (BLK, HD), kind)

    gather_sems = [
        dma((count * HALVES,)) for count in (5, LINE, LINE, LINE, 2 * LINE, 2 * LINE)
    ]
    scatter_parts = [
        tiles(2 * LINE, ROWS, kind=wide),
        tiles(2 * LINE, ROWS),
        tiles(2 * LINE, ROWS),
        tiles(LINE, ROWS),
        tiles(LINE, ROWS),
        tiles(LINE - 1, ROWS),
        tiles(5, ROWS),
    ] + [dma((count,)) for count in (2 * LINE, 2 * LINE, LINE, LINE, LINE - 1, 5)]
    return pl.pallas_call(
        fused_kernel,
        in_specs=[smem, smem, vmem, hbm, hbm, hbm, hbm],
        out_specs=[vmem] * 4,
        out_shape=[
            jax.ShapeDtypeStruct((ROWS * BLK, HQ * HD), half),
            jax.ShapeDtypeStruct((ROWS * BLK, HQ * HD), half),
            jax.ShapeDtypeStruct(keys.shape, half),
            jax.ShapeDtypeStruct(keys.shape, half),
        ],
        scratch_shapes=[
            tiles(total_blocks),
            tiles(total_blocks),
            tiles(total_blocks),
            tiles(total_blocks),
            tiles(ROWS, HQ),
            tiles(ROWS, HQ),
            pltpu.VMEM((ROWS, 5, BLK, HQ * BLK), half),
            tiles(PICKS),
            tiles(PICKS),
            tiles(ROWS + 2, kind=wide),
            tiles(G, kind=wide),
            tiles(EACH + 1, kind=wide),
            tiles(ROWS, kind=wide),
            pltpu.VMEM((8, BLK), jnp.int32),
            pltpu.SMEM((8, BLK), jnp.int32),
            dma((3 + 2 * HQ,)),
        ]
        + gather_sems * 2
        + scatter_parts * 2,
        compiler_params=pltpu.CompilerParams(
            collective_id=0, has_side_effects=True, vmem_limit_bytes=FUSED_MIB * 1024 * 1024
        ),
        name="fused_attention",
    )(random_ids, global_ids, segments, queries, out_grads, keys, values)


FUSED_MIB = 52


def fused_body(queries, key_rows, value_rows, out_grads, segment_ids, random_blocks, global_blocks):
    total_blocks = segment_ids.shape[0] // BLK

    def blocks(array):
        return array.reshape(ROWS, BLK, -1)

    attended, query_grads, key_grads, value_grads = fused_call(
        random_blocks.transpose(2, 0, 1),
        global_blocks,
        segment_ids.reshape(total_blocks, BLK),
        blocks(queries),
        blocks(out_grads),
        blocks(key_rows),
        blocks(value_rows),
    )
    return (attended, query_grads, key_grads.reshape(-1, HD), value_grads.reshape(-1, HD))


def plan(*arrays):
    tokens = arrays[4].shape[0]
    fits = tokens * 2 * HD * 4 <= DENSE_BYTES
    chosen = fused_body if fits and arrays[0].shape[0] == ROWS * BLK and lax.axis_size("seq") == SEQ else body
    return chosen(*arrays)


def solution(mesh):
    placed = (
        P(("shard", "seq"), None),
        P(("shard", "seq"), None),
        P(("shard", "seq"), None),
        P(("shard", "seq"), None),
        P("shard"),
        P(("shard", "seq"), None, None),
        P("shard"),
    )
    return jax.shard_map(
        plan,
        mesh=mesh,
        in_specs=placed,
        out_specs=(
            P(("shard", "seq"), None),
            P(("shard", "seq"), None),
            P(("shard", "seq"), None),
            P(("shard", "seq"), None),
        ),
        check_vma=False,
    )
```

```python
import math

import jax
import jax.numpy as jnp
from jax import lax
from jax.experimental import pallas as pl
from jax.experimental.pallas import tpu as pltpu
from jax.sharding import PartitionSpec as P

HD = 128
HQ = 8
BLK = 128
RAND = 3
G = 2


masked_value = -1e30


def with_halo(array, sides, width):
    for axis, dim in sides:
        size, length = (lax.axis_size(axis), array.shape[dim])
        up = [(i, (i + 1) % size) for i in range(size - 1)]
        down = [(j, i) for i, j in up]
        last = lax.slice_in_dim(array, length - width, length, axis=dim)
        first = lax.slice_in_dim(array, 0, width, axis=dim)
        before = lax.ppermute(last, axis, up)
        after = lax.ppermute(first, axis, down)
        array = jnp.concatenate([before, array, after], axis=dim)
    return array


def spread(block, axis, owner):
    block = jnp.where(lax.axis_index(axis) == owner, block, jnp.zeros_like(block))
    return lax.psum(block, axis)


def from_behind(block, axis, distance):
    devices = range(lax.axis_size(axis))
    route = [(i - distance, i) for i in devices if i - distance in devices]
    return lax.ppermute(block, axis, route)


def routing(block_ids, per_device):
    owners = block_ids // per_device
    ordering = jnp.arange(block_ids.shape[0])
    earlier = (owners[:, None] == owners[None, :]) & (ordering[None, :] < ordering[:, None])
    return (owners, jnp.sum(earlier.astype(jnp.int32), axis=1))


def taken(blocks, indices):
    return lax.map(lambda i: lax.dynamic_index_in_dim(blocks, i, 0, keepdims=False), indices)


def block_pass(
    query_block,
    grad_block,
    shared,
    shared_live,
    query_segs,
    shared_segs,
    random_kv,
    random_segs,
    scaling,
):
    wide = jnp.float32
    shared_mask = (query_segs[:, None, None] == shared_segs[None]) & shared_live[None, :, None]
    random_mask = query_segs[None, :, None, None] == random_segs[:, None]
    shared_scores = (
        jnp.einsum("thd,jkd->htjk", query_block, shared[:, :, :HD], preferred_element_type=wide)
        * scaling
    )
    shared_scores = jnp.where(shared_mask[None], shared_scores, masked_value)
    random_scores = (
        jnp.einsum(
            "thd,hrkd->htrk", query_block, random_kv[:, :, :, :HD], preferred_element_type=wide
        )
        * scaling
    )
    random_scores = jnp.where(random_mask, random_scores, masked_value)
    top_score = jnp.maximum(
        jnp.max(shared_scores, axis=(2, 3)), jnp.max(random_scores, axis=(2, 3))
    )
    totals = jnp.sum(jnp.exp(shared_scores - top_score[:, :, None, None]), axis=(2, 3))
    totals = totals + jnp.sum(jnp.exp(random_scores - top_score[:, :, None, None]), axis=(2, 3))
    log_totals = top_score + jnp.log(totals)
    shared_probs = jnp.exp(shared_scores - log_totals[:, :, None, None])
    random_probs = jnp.exp(random_scores - log_totals[:, :, None, None])
    shared_half = shared_probs.astype(jnp.bfloat16)
    random_half = random_probs.astype(jnp.bfloat16)
    attended = jnp.einsum(
        "htjk,jkd->thd", shared_half, shared[:, :, HD:], preferred_element_type=wide
    )
    attended = attended + jnp.einsum(
        "htrk,hrkd->thd", random_half, random_kv[:, :, :, HD:], preferred_element_type=wide
    )
    attended = attended.astype(jnp.bfloat16)
    row_dots = jnp.einsum("thd,thd->ht", grad_block, attended, preferred_element_type=wide)
    shared_dprobs = jnp.einsum(
        "thd,jkd->htjk", grad_block, shared[:, :, HD:], preferred_element_type=wide
    )
    random_dprobs = jnp.einsum(
        "thd,hrkd->htrk", grad_block, random_kv[:, :, :, HD:], preferred_element_type=wide
    )
    shared_dscores = (shared_probs * (shared_dprobs - row_dots[:, :, None, None])).astype(
        jnp.bfloat16
    )
    random_dscores = (random_probs * (random_dprobs - row_dots[:, :, None, None])).astype(
        jnp.bfloat16
    )
    query_grads = jnp.einsum(
        "htjk,jkd->thd", shared_dscores, shared[:, :, :HD], preferred_element_type=wide
    )
    query_grads = query_grads + jnp.einsum(
        "htrk,hrkd->thd", random_dscores, random_kv[:, :, :, :HD], preferred_element_type=wide
    )
    query_grads = (query_grads * scaling).astype(jnp.bfloat16)
    shared_kgrad = (
        jnp.einsum("htjk,thd->jkd", shared_dscores, query_block, preferred_element_type=wide)
        * scaling
    )
    shared_vgrad = jnp.einsum("htjk,thd->jkd", shared_half, grad_block, preferred_element_type=wide)
    shared_grads = jnp.where(
        shared_live[:, None, None], jnp.concatenate([shared_kgrad, shared_vgrad], axis=2), 0.0
    )
    random_kgrad = (
        jnp.einsum("htrk,thd->hrkd", random_dscores, query_block, preferred_element_type=wide)
        * scaling
    )
    random_vgrad = jnp.einsum(
        "htrk,thd->hrkd", random_half, grad_block, preferred_element_type=wide
    )
    random_grads = jnp.concatenate([random_kgrad, random_vgrad], axis=3)
    return (attended, query_grads, shared_grads, random_grads, log_totals, row_dots)


def body(queries, key_rows, value_rows, out_grads, segment_ids, random_blocks, global_blocks):
    scaling = 1.0 / math.sqrt(HD)
    row_count = queries.shape[0]
    qcount = row_count // BLK
    devices = lax.axis_size("seq")
    position = lax.axis_index("seq")
    total_blocks = segment_ids.shape[0] // BLK
    seg_blocks = segment_ids.reshape(total_blocks, BLK)
    joined = jnp.concatenate([key_rows, value_rows], axis=1)
    local_blocks = joined.reshape(qcount, BLK, 2 * HD)
    padded = with_halo(joined, (("seq", 0),), BLK)
    owned = global_blocks // qcount == position
    pieces = []
    for global_slot in range(G):
        picked = lax.dynamic_index_in_dim(
            local_blocks, global_blocks[global_slot] % qcount, 0, keepdims=False
        )
        pieces.append(spread(picked, "seq", global_blocks[global_slot] // qcount))
    global_kv = jnp.stack(pieces)
    chosen_ids = random_blocks.reshape(-1)
    pick_count = chosen_ids.shape[0]
    capacity = -(-pick_count // devices)
    owners, slots = routing(chosen_ids, qcount)
    outgoing_ids = (
        jnp.full((devices, capacity), -1, jnp.int32).at[owners, slots].set(chosen_ids % qcount)
    )
    wanted = lax.all_to_all(outgoing_ids, "seq", split_axis=0, concat_axis=0, tiled=True)
    wanted_clip = jnp.clip(wanted, 0, qcount - 1)
    served = taken(local_blocks, wanted_clip.reshape(-1)).reshape(wanted.shape + (BLK, 2 * HD))
    answer = lax.all_to_all(served, "seq", split_axis=0, concat_axis=0, tiled=True)
    answer = answer.reshape(devices * capacity, BLK, 2 * HD)
    random_kv = taken(answer, owners * capacity + slots)
    random_kv = random_kv.reshape(qcount, HQ, RAND, BLK, 2 * HD)
    query_blocks = queries.reshape(qcount, BLK, HQ, HD)
    grad_blocks = out_grads.reshape(qcount, BLK, HQ, HD)

    def attend(bundle):
        block_index, query_block, grad_block, block_kv, block_ids = bundle
        global_index = position * qcount + block_index
        window = lax.dynamic_slice_in_dim(padded, block_index * BLK, 3 * BLK, 0).reshape(
            3, BLK, 2 * HD
        )
        window_ids = global_index + jnp.arange(-1, 2, dtype=jnp.int32)
        window_live = (window_ids >= 0) & (window_ids < total_blocks)
        shared_ids = jnp.concatenate([jnp.clip(window_ids, 0, total_blocks - 1), global_blocks])
        shared_live = jnp.concatenate([window_live, jnp.ones((G,), bool)])
        shared = jnp.concatenate([window, global_kv], axis=0)
        return block_pass(
            query_block,
            grad_block,
            shared,
            shared_live,
            seg_blocks[global_index],
            seg_blocks[shared_ids],
            block_kv,
            seg_blocks[block_ids],
            scaling,
        )

    attended, query_grads, shared_grads, random_grads, log_totals, row_dots = lax.map(
        attend,
        (jnp.arange(qcount, dtype=jnp.int32), query_blocks, grad_blocks, random_kv, random_blocks),
    )
    window_sum = jnp.zeros((qcount + 2, BLK, 2 * HD), jnp.float32)
    for offset in range(3):
        window_sum = window_sum.at[offset : offset + qcount].add(shared_grads[:, offset])
    from_right = from_behind(window_sum[0].astype(jnp.bfloat16), "seq", -1).astype(jnp.float32)
    from_left = from_behind(window_sum[qcount + 1].astype(jnp.bfloat16), "seq", 1).astype(
        jnp.float32
    )
    own_grads = window_sum[1 : qcount + 1]
    own_grads = own_grads.at[qcount - 1].add(from_right).at[0].add(from_left)
    global_sum = lax.psum(jnp.sum(shared_grads[:, 3:], axis=0), "seq")
    global_hits = (
        (global_blocks[:, None] % qcount == jnp.arange(qcount)[None, :]) & owned[:, None]
    ).astype(jnp.float32)
    own_grads = own_grads + jnp.einsum(
        "gq,gkd->qkd", global_hits, global_sum, precision=lax.Precision.HIGHEST
    )
    outgoing = (
        jnp.zeros((devices, capacity, BLK, 2 * HD), jnp.float32)
        .at[owners, slots]
        .set(random_grads.reshape(pick_count, BLK, 2 * HD))
    )
    returned = lax.all_to_all(outgoing, "seq", split_axis=0, concat_axis=0, tiled=True)
    request_hits = (wanted[:, :, None] == jnp.arange(qcount)[None, None, :]).astype(jnp.float32)
    own_grads = own_grads + jnp.einsum(
        "ncq,nckd->qkd", request_hits, returned, precision=lax.Precision.HIGHEST
    )
    own_flat = own_grads.reshape(row_count, 2 * HD)
    return (
        attended.reshape(row_count, HQ * HD),
        query_grads.reshape(row_count, HQ * HD),
        own_flat[:, :HD].astype(jnp.bfloat16),
        own_flat[:, HD:].astype(jnp.bfloat16),
    )


LOG2E = 1.4426950408889634
DENSE_BYTES = 16 * 1024 * 1024
LINE = 4
SEQ = 16


class Place:
    def __init__(self):
        me = lax.axis_index("seq")
        self.me = me
        self.core = lax.rem(me, 2)
        self.x = lax.rem(me // 2, 2)
        self.z = me // 4
        self.high = self.z // 2
        self.step = 1 - 2 * self.high
        self.inner = jnp.where((self.z == 1) | (self.z == 2), 1, 0)
        self.partner = self.at(self.z, self.x, 1 - self.core)
        self.across = self.at(self.z, 1 - self.x, self.core)
        self.onward = self.at(self.z + self.step, self.x, self.core)
        self.outward = self.at(self.z - self.step, self.x, self.core)

    def at(self, z, x, core):
        return z * 4 + x * 2 + core


def greet(place):
    barrier = pltpu.get_barrier_semaphore()
    for other in (place.partner, place.across, place.onward):
        pl.semaphore_signal(
            barrier, inc=1, device_id={"seq": other}, device_id_type=pl.DeviceIdType.MESH
        )

    @pl.when(place.inner == 1)
    def _():
        pl.semaphore_signal(
            barrier, inc=1, device_id={"seq": place.outward}, device_id_type=pl.DeviceIdType.MESH
        )

    pl.semaphore_wait(barrier, 3 + place.inner)


def remote(source, target, send, receive, device):
    return pltpu.make_async_remote_copy(
        src_ref=source,
        dst_ref=target,
        send_sem=send,
        recv_sem=receive,
        device_id={"seq": device},
        device_id_type=pl.DeviceIdType.MESH,
    )


ROWS = 4
PICKS = ROWS * HQ * RAND
EACH = PICKS // SEQ
HALVES = 2


class Gather:
    def __init__(self, place, buffer, zs, zr, xs, xr, cs, cr):
        self.place = place
        z, step, inner = place.z, place.step, place.inner
        lines = [z, z + step - 2 * step * inner, z + step * (2 - inner), z + step * (3 - inner)]
        self.own = [place.at(line, place.x, place.core) for line in lines]
        self.other = [place.at(line, 1 - place.x, place.core) for line in lines]
        self.own_far = [place.at(line, place.x, 1 - place.core) for line in lines]
        self.other_far = [place.at(line, 1 - place.x, 1 - place.core) for line in lines]
        width = ROWS // HALVES

        def copies(owner, sends, at, receives, to, device):
            made = []
            for half in range(HALVES):
                part = buffer.at[pl.ds(owner * ROWS + half * width, width)]
                made.append(
                    remote(
                        part,
                        part,
                        sends.at[at * HALVES + half],
                        receives.at[to * HALVES + half],
                        device,
                    )
                )
            return made

        onward, outward = place.onward, place.outward
        own, other = self.own, self.other
        self.edge = copies(own[0], zs, 0, zr, 1, onward)
        self.along = copies(own[0], zs, 0, zr, 2, onward)
        self.out = copies(own[0], zs, 1, zr, 1, outward)
        self.relays = [
            copies(own[1], zs, 2, zr, 3, onward),
            copies(own[2], zs, 3, zr, 2, outward),
            copies(own[3], zs, 4, zr, 3, outward),
        ]
        self.arrivals = [copies(own[k], zs, 0, zr, k, onward) for k in range(LINE)]
        self.crossing = [copies(own[k], xs, k, xr, k, place.across) for k in range(LINE)]
        self.crossed = [copies(other[k], xs, k, xr, k, place.across) for k in range(LINE)]
        self.near = [copies(own[k], cs, k, cr, k, place.partner) for k in range(LINE)]
        self.far = [copies(other[k], cs, LINE + k, cr, LINE + k, place.partner) for k in range(LINE)]

    def start_line(self):
        @pl.when(self.place.inner == 0)
        def _():
            for copy in self.edge:
                copy.start()

        @pl.when(self.place.inner == 1)
        def _():
            for half in range(HALVES):
                self.out[half].start()
                self.along[half].start()

    def start_cross(self):
        for half in range(HALVES):
            self.crossing[0][half].start()
            self.near[0][half].start()

    def line_arrival(self, k, cross=True):
        for half in range(HALVES):
            self.arrivals[k][half].wait_recv()

            @pl.when(self.place.inner == 1)
            def _(half=half):
                self.relays[k - 1][half].start()

            if cross:
                self.crossing[k][half].start()
            self.near[k][half].start()

    def cross_late(self, k):
        for half in range(HALVES):
            self.crossing[k][half].start()

    def cross_arrival(self, k):
        for half in range(HALVES):
            self.crossed[k][half].wait_recv()
            self.far[k][half].start()

    def near_arrival(self, k):
        for half in range(HALVES):
            self.near[k][half].wait_recv()

    def far_arrival(self, k):
        for half in range(HALVES):
            self.far[k][half].wait_recv()

    def wait_sends(self):
        for half in range(HALVES):
            self.edge[half].wait_send()
            for k in range(LINE):
                self.crossing[k][half].wait_send()
                self.near[k][half].wait_send()
                self.far[k][half].wait_send()

        @pl.when(self.place.inner == 1)
        def _():
            for half in range(HALVES):
                self.out[half].wait_send()
                for relay in self.relays:
                    relay[half].wait_send()


class Scatter:
    def __init__(
        self, place, kept, pair_out, pair_in, cross_out, cross_in, line_out, line_in,
        ps, pr, xs, xr, zs, zr,
    ):
        self.place = place
        self.kept, self.pair_out, self.pair_in = kept, pair_out, pair_in
        self.cross_out, self.cross_in = cross_out, cross_in
        self.line_out, self.line_in = line_out, line_in
        self.sems = (ps, pr, xs, xr, zs, zr)
        z, high = place.z, place.high
        self.order = [3 * (1 - high), 2 - high, 1 - z + 4 * high, z]

    def pair(self, index):
        ps, pr = self.sems[:2]
        return remote(
            self.pair_out.at[index], self.pair_in.at[index], ps.at[index], pr.at[index],
            self.place.partner,
        )

    def cross(self, k, half):
        xs, xr = self.sems[2:4]
        at = k * HALVES + half
        return remote(
            self.cross_out.at[k, part(half)], self.cross_in.at[k, part(half)], xs.at[at],
            xr.at[at], self.place.across,
        )

    def hop(self, k, slot, half, device):
        zs, zr = self.sems[4:]
        return remote(
            self.line_out.at[k, part(half)], self.line_in.at[slot, part(half)],
            zs.at[k * HALVES + half], zr.at[slot * HALVES + half], device,
        )

    def start_cross(self, k):
        self.pair(2 * k).wait_recv()
        for half in range(HALVES):
            total = self.kept[2 * k, part(half)] + self.pair_in[2 * k, part(half)].astype(jnp.float32)
            self.cross_out[k, part(half)] = total.astype(jnp.bfloat16)
            self.cross(k, half).start()

    def local(self, k, half):
        wide = jnp.float32
        self.cross(k, half).wait_recv()
        total = self.kept[2 * k + 1, part(half)] + self.pair_in[2 * k + 1, part(half)].astype(wide)
        return total + self.cross_in[k, part(half)].astype(wide)

    def arrived(self, slot, half):
        self.hop(0, slot, half, self.place.onward).wait_recv()
        return self.line_in[slot, part(half)].astype(jnp.float32)

    def edge_hop(self, k):
        self.pair(2 * k + 1).wait_recv()
        for half in range(HALVES):
            self.line_out[k, part(half)] = self.local(k, half).astype(jnp.bfloat16)
            self.hop(k, k, half, self.place.onward).start()

    def inner_hop(self, k):
        self.pair(2 * k + 1).wait_recv()
        for half in range(HALVES):
            total = self.local(k, half) + self.arrived(k if k < 2 else 3, half)
            self.line_out[k, part(half)] = total.astype(jnp.bfloat16)
            if k < 2:
                self.hop(k, 3 + k, half, self.place.onward).start()
            else:
                self.hop(k, 0, half, self.place.outward).start()

    def finish(self, result, slots):
        k = LINE - 1
        self.pair(2 * k + 1).wait_recv()
        for half in range(HALVES):
            total = self.local(k, half)
            for slot in slots:
                total = total + self.arrived(slot, half)
            result[part(half)] = total.astype(result.dtype)

    def edge_finish(self, result):
        self.finish(result, (0,))

    def inner_finish(self, result):
        self.finish(result, (2, 4))

    def wait_sends(self):
        for index in range(2 * LINE):
            self.pair(index).wait_send()
        for half in range(HALVES):
            for k in range(LINE):
                self.cross(k, half).wait_send()
            for k in range(LINE - 1):
                self.hop(k, k, half, self.place.onward).wait_send()


def part(half):
    return pl.ds(half * (ROWS // HALVES), ROWS // HALVES)


def pick_table(random_ref, table_ref):
    shape = (BLK, BLK)
    lane = lax.broadcasted_iota(jnp.int32, shape, 1)
    row = lax.broadcasted_iota(jnp.int32, shape, 0)
    far = 1 << 20
    by_lane = jnp.full((8, BLK), far, jnp.int32)
    small = lax.broadcasted_iota(jnp.int32, (8, BLK), 1)
    by_row = jnp.full(shape, far, jnp.int32)
    for pick in range(PICKS):
        name = random_ref[pick % RAND, pick // (HQ * RAND), pick // RAND % HQ]
        by_lane = jnp.where(small == pick, name * BLK, by_lane)
        by_row = jnp.where(row == pick, name * BLK, by_row)
    by_lane = by_lane + small
    by_row = by_row + row
    rank = jnp.sum((by_lane[0:1] < by_row).astype(jnp.int32), axis=1, keepdims=True)
    code = row * 64 + ((row * 171) >> 9)
    ordered = jnp.sum(jnp.where(rank == lane, code, 0), axis=0, keepdims=True)
    before = jnp.sum((by_row < lane * BLK).astype(jnp.int32), axis=0, keepdims=True)
    table_ref[0:1] = ordered
    table_ref[1:2] = before


def against(rows, columns):
    return lax.dot_general(
        rows, columns, (((1,), (1,)), ((), ())), preferred_element_type=jnp.float32
    )


def product(rows, columns):
    return jnp.dot(rows, columns, preferred_element_type=jnp.float32)


def names_of(mine, block, random_ref, global_ref, total_blocks):
    shared_ids = [
        jnp.maximum(mine - 1, 0),
        mine,
        jnp.minimum(mine + 1, total_blocks - 1),
        global_ref[0],
        global_ref[1],
    ]
    random_ids = [[random_ref[pick, block, head] for pick in range(RAND)] for head in range(HQ)]
    return shared_ids, random_ids


def add_shared(block, tiles, stack, window_ref, global_sum_ref):
    sums = product(jnp.concatenate(tiles[:5], axis=0), stack)
    for slot in range(3):
        window_ref[block + slot] += sums[span(slot)]
    for slot in range(G):
        global_sum_ref[1 + slot] += sums[span(3 + slot)]


def span(head):
    return slice(head * BLK, (head + 1) * BLK)


def key_flags(boundary, name):
    shape = (BLK, HD)
    row = lax.broadcasted_iota(jnp.int32, shape, 0)
    lane = lax.broadcasted_iota(jnp.int32, shape, 1)
    low = row < boundary - name * BLK
    one = jnp.where((lane == 0) & low, 1.0, 0.0) + jnp.where(lane == 1, 1.0, 0.0)
    return (one - jnp.where((lane == 1) & low, 1.0, 0.0)).astype(jnp.bfloat16)


def query_flags(boundary, name):
    shape = (BLK, HD)
    row = lax.broadcasted_iota(jnp.int32, shape, 0)
    lane = lax.broadcasted_iota(jnp.int32, shape, 1)
    low = row < boundary - name * BLK
    one = jnp.where((lane == 1) & low, masked_value, 0.0)
    two = jnp.where(lane == 0, masked_value, 0.0) - jnp.where((lane == 0) & low, masked_value, 0.0)
    return (one + two).astype(jnp.bfloat16)


def split(shared, picked):
    tiles = [shared[span(slot)] for slot in range(5)]
    for pick in range(RAND):
        tiles.append(jnp.concatenate([part[span(pick)] for part in picked], axis=1))
    return tiles


def score_block(
    block, mine, boundary, random_ref, global_ref, query_ref, grad_ref, key_ref, flag_ref,
    shared_ref, picked_ref, inverse_ref, window_ref, global_sum_ref,
):
    half = jnp.bfloat16
    total_blocks = key_ref.shape[0]
    shared_ids, random_ids = names_of(mine, block, random_ref, global_ref, total_blocks)
    flag_ids = list(shared_ids)
    flag_ids[0] = jnp.where(mine == 0, total_blocks, flag_ids[0])
    flag_ids[2] = jnp.where(mine == total_blocks - 1, total_blocks, flag_ids[2])

    def flagged(ids, flag_ids):
        return jnp.concatenate(
            [jnp.concatenate([key_ref[i], flag_ref[j]], axis=1) for i, j in zip(ids, flag_ids)],
            axis=0,
        )

    mark = query_flags(boundary, mine)
    factor = LOG2E / math.sqrt(HD)
    marked = [jnp.concatenate([query_ref[block, head], mark], axis=1) for head in range(HQ)]
    stack = jnp.concatenate(marked, axis=0)
    shared = against(flagged(shared_ids, flag_ids), stack)
    picked = [
        against(flagged(random_ids[head], random_ids[head]), marked[head]) for head in range(HQ)
    ]
    scores = split(shared, picked)
    top = scores[0]
    for tile in scores[1:]:
        top = jnp.maximum(top, tile)
    top = jnp.max(top, axis=0, keepdims=True) * factor
    powers = [jnp.exp2(tile * factor - top) for tile in scores]
    total = powers[0]
    for tile in powers[1:]:
        total = total + tile
    inverse = 1.0 / jnp.sum(total, axis=0, keepdims=True)
    powers = [tile.astype(half) for tile in powers]
    for slot in range(5):
        shared_ref[block, slot] = powers[slot]
    for pick in range(RAND):
        for head in range(HQ):
            picked_ref[(block * HQ + head) * RAND + pick] = powers[5 + pick][:, span(head)]
    inverse_ref[block, 0:1] = inverse
    scaled = []
    for head in range(HQ):
        turned = jnp.broadcast_to(inverse[:, span(head)], (BLK, BLK)).T
        scaled.append((grad_ref[block, head].astype(jnp.float32) * turned).astype(half))
        grad_ref[block, head] = scaled[head]
    add_shared(block, powers, jnp.concatenate(scaled, axis=0), window_ref, global_sum_ref)


def entries(source, shared_ids, random_ids, parts):
    def stacked(ids):
        return jnp.concatenate([source[i] for i in ids], axis=0)

    shared = against(stacked(shared_ids), jnp.concatenate(parts, axis=0))
    return split(shared, [against(stacked(random_ids[head]), parts[head]) for head in range(HQ)])


def gathered(turned, shared_ids, random_ids, tiles):
    shared = product(
        jnp.concatenate([turned[i] for i in shared_ids], axis=1),
        jnp.concatenate(tiles[:5], axis=0),
    )
    pieces = []
    for head in range(HQ):
        pieces.append(
            product(
                jnp.concatenate([turned[i] for i in random_ids[head]], axis=1),
                jnp.concatenate([tile[:, span(head)] for tile in tiles[5:]], axis=0),
            )
        )
    return shared + jnp.concatenate(pieces, axis=1)


def grad_block(
    block, mine, random_ref, global_ref, query_ref, grad_ref, value_ref, key_turned, value_turned,
    shared_ref, picked_ref, dpicked_ref, inverse_ref, window_ref, global_sum_ref,
    attended_ref, query_grad_ref,
):
    wide = jnp.float32
    half = jnp.bfloat16
    total_blocks = value_ref.shape[0]
    shared_ids, random_ids = names_of(mine, block, random_ref, global_ref, total_blocks)
    queries = [query_ref[block, head] for head in range(HQ)]
    grads = [grad_ref[block, head] for head in range(HQ)]
    probs = [shared_ref[block, slot] for slot in range(5)]
    for pick in range(RAND):
        probs.append(
            jnp.concatenate(
                [picked_ref[(block * HQ + head) * RAND + pick] for head in range(HQ)], axis=1
            )
        )
    attended = gathered(value_turned, shared_ids, random_ids, probs) * inverse_ref[block, 0:1]
    attended = attended.astype(half).astype(wide)
    grads_turned = jnp.concatenate([part.astype(wide).T for part in grads], axis=1)
    row_dots = jnp.sum(attended * grads_turned, axis=0, keepdims=True)
    for head in range(HQ):
        attended_ref[block, :, span(head)] = attended[:, span(head)].T.astype(half)
    dprobs = entries(value_ref, shared_ids, random_ids, grads)
    dscores = [(p.astype(wide) * (d - row_dots)).astype(half) for p, d in zip(probs, dprobs)]
    for pick in range(RAND):
        for head in range(HQ):
            dpicked_ref[(block * HQ + head) * RAND + pick] = dscores[5 + pick][:, span(head)]
    add_shared(block, dscores, jnp.concatenate(queries, axis=0), window_ref, global_sum_ref)
    query_grads = gathered(key_turned, shared_ids, random_ids, dscores) * (1.0 / math.sqrt(HD))
    for head in range(HQ):
        query_grad_ref[block, :, span(head)] = query_grads[:, span(head)].T.astype(half)


def sum_owner(
    index, scatter, scale, table, global_ref, tiles_ref, rows_ref, window_ref, global_sum_ref,
    running_ref, owner_ref,
):
    place = scatter.place
    k, turn = index // 4, lax.rem(index, 4)
    side, kind = lax.rem(turn, 2), turn // 2
    line = scatter.order[3]
    for other in (2, 1, 0):
        line = jnp.where(k == other, scatter.order[other], line)
    x = jnp.where(side == 0, 1 - place.x, place.x)
    core = jnp.where(kind == 0, 1 - place.core, place.core)
    owner = place.at(line, x, core)
    running = None
    for pick in range(EACH):
        code = table[0, owner * EACH + pick]
        term = product(tiles_ref[code >> 6], rows_ref[(code >> 3) & 7, code & 7])
        running = term if running is None else running + term
        running_ref[pick + 1] = running
    for row in range(ROWS):
        name = owner * ROWS + row
        first = jnp.clip(table[1, name] - owner * EACH, 0, EACH)
        last = jnp.clip(table[1, name + 1] - owner * EACH, 0, EACH)
        hit = jnp.where(global_ref[0] == name, 1, 0) + jnp.where(global_ref[1] == name, 2, 0)
        owner_ref[row] = running_ref[last] - running_ref[first] + global_sum_ref[hit]

    @pl.when(owner == place.me)
    def _():
        for row in range(ROWS):
            owner_ref[row] += window_ref[1 + row]

    @pl.when(owner == place.me - 1)
    def _():
        owner_ref[ROWS - 1] += window_ref[0]

    @pl.when(owner == place.me + 1)
    def _():
        owner_ref[0] += window_ref[ROWS + 1]

    slot = 2 * k + side

    @pl.when(kind == 0)
    def _():
        scatter.pair_out[slot] = (owner_ref[...] * scale).astype(jnp.bfloat16)
        scatter.pair(slot).start()

    @pl.when(kind == 1)
    def _():
        scatter.kept[slot] = owner_ref[...] * scale


def fused_kernel(
    random_ref, global_ref, segment_in, query_in, grad_in, key_in, value_in,
    attended_out, query_grad_out, key_grad_out, value_grad_out,
    keys, values, key_turned, value_turned, queries, grads, flag_ref, shared_ref, picked_ref,
    dpicked_ref, inverse_ref, window_ref, global_sum_ref, running_ref, owner_ref, table_vec, table, segment_ref,
    attended_ref, query_grad_ref, key_grad_ref, value_grad_ref, local_sems, out_sems,
    *rest,
):
    place = Place()
    wide = jnp.float32
    total_blocks = keys.shape[0]
    key_sems, value_sems, rest = rest[:6], rest[6:12], rest[12:]
    value_scatter = Scatter(place, *rest[:13])
    key_scatter = Scatter(place, *rest[13:])
    me = place.me
    first = me * ROWS
    own = pl.ds(first, ROWS)
    loads = [
        pltpu.make_async_copy(key_in, keys.at[own], local_sems.at[0]),
        pltpu.make_async_copy(value_in, values.at[own], local_sems.at[1]),
        pltpu.make_async_copy(segment_in, segment_ref, local_sems.at[3 + 2 * HQ]),
    ]
    for head in range(HQ):
        span = pl.ds(head * HD, HD)
        loads.append(
            pltpu.make_async_copy(
                query_in.at[:, :, span], queries.at[:, head], local_sems.at[2 + head]
            )
        )
        loads.append(
            pltpu.make_async_copy(
                grad_in.at[:, :, span], grads.at[:, head], local_sems.at[2 + HQ + head]
            )
        )
    for load in loads:
        load.start()
    greet(place)
    for load in loads[:3]:
        load.wait()
    key_gather = Gather(place, keys, *key_sems)
    value_gather = Gather(place, values, *value_sems)

    def turn(source, target, owner):
        for row in range(ROWS):
            target[owner * ROWS + row] = source[owner * ROWS + row].T

    def turn_keys(owner):
        turn(keys, key_turned, owner)

    def turn_values(owner):
        turn(values, value_turned, owner)

    key_gather.start_line()
    value_gather.start_line()
    key_gather.start_cross()
    value_gather.start_cross()
    pick_table(random_ref, table_vec)
    table_copy = pltpu.make_async_copy(table_vec, table, local_sems.at[2 + 2 * HQ])
    table_copy.start()
    zero = jnp.zeros((BLK, HD), wide)

    def clear():
        for row in range(ROWS + 2):
            window_ref[row] = zero
        for slot in range(G + 2):
            global_sum_ref[slot] = zero

    clear()
    running_ref[0] = zero
    boundary = jnp.sum((segment_ref[...] == segment_ref[0:1, 0:1]).astype(jnp.int32))
    @pl.loop(0, total_blocks)
    def _(name):
        flag_ref[name] = key_flags(boundary, name)

    flag_ref[total_blocks] = jnp.where(
        lax.broadcasted_iota(jnp.int32, (BLK, HD), 1) < 2, 1.0, 0.0
    ).astype(jnp.bfloat16)
    key_gather.line_arrival(1)
    key_gather.cross_arrival(0)
    turn_keys(key_gather.own[0])
    turn_values(key_gather.own[0])
    key_gather.line_arrival(2)
    value_gather.cross_arrival(0)
    turn_keys(key_gather.own[1])
    turn_keys(key_gather.other[0])
    key_gather.cross_arrival(1)
    value_gather.line_arrival(1, cross=False)
    turn_values(value_gather.own[1])
    turn_values(value_gather.other[0])
    key_gather.line_arrival(3)
    value_gather.cross_late(1)
    turn_keys(key_gather.own[2])
    turn_keys(key_gather.other[1])
    value_gather.line_arrival(2)
    turn_keys(key_gather.own[3])
    turn_values(value_gather.own[2])
    key_gather.cross_arrival(2)
    turn_keys(key_gather.other[2])
    value_gather.line_arrival(3)
    turn_values(value_gather.own[3])
    for k in range(LINE - 1):
        key_gather.near_arrival(k)
        turn_keys(key_gather.own_far[k])
        key_gather.far_arrival(k)
        turn_keys(key_gather.other_far[k])
    key_gather.cross_arrival(3)
    turn_keys(key_gather.other[3])
    key_gather.near_arrival(3)
    turn_keys(key_gather.own_far[3])
    for load in loads[3:]:
        load.wait()
    table_copy.wait()
    key_gather.far_arrival(3)
    turn_keys(key_gather.other_far[3])

    @pl.loop(0, ROWS)
    def _(block):
        score_block(
            block, first + block, boundary, random_ref, global_ref, queries, grads, keys,
            flag_ref, shared_ref, picked_ref, inverse_ref, window_ref, global_sum_ref,
        )
        for k in range(1, LINE):

            @pl.when(block == k - 1)
            def _(k=k):
                value_gather.cross_arrival(k)
                turn_values(value_gather.other[k])
                value_gather.near_arrival(k)
                turn_values(value_gather.own_far[k])

    def owners(scatter, scale, tiles_ref, rows_ref, events):
        global_sum_ref[3] = global_sum_ref[1] + global_sum_ref[2]

        @pl.loop(0, SEQ)
        def _(index):
            sum_owner(
                index, scatter, scale, table, global_ref, tiles_ref, rows_ref, window_ref,
                global_sum_ref, running_ref, owner_ref,
            )
            for k in range(LINE - 1):

                @pl.when(index == 4 * k + 7)
                def _(k=k):
                    scatter.start_cross(k)
                    events(k)

        scatter.start_cross(LINE - 1)

    owners(value_scatter, 1.0, picked_ref, grads, lambda k: None)
    clear()
    value_gather.near_arrival(0)
    turn_values(value_gather.own_far[0])
    for k in range(LINE):
        value_gather.far_arrival(k)
        turn_values(value_gather.other_far[k])
    edge, inner = place.inner == 0, place.inner == 1

    def block_out(block):
        return [
            pltpu.make_async_copy(source.at[block], target.at[block], out_sems.at[at * ROWS + block])
            for at, (source, target) in enumerate(
                [(attended_ref, attended_out), (query_grad_ref, query_grad_out)]
            )
        ]

    value_out = pltpu.make_async_copy(value_grad_ref, value_grad_out, out_sems.at[2 * ROWS])
    key_out = pltpu.make_async_copy(key_grad_ref, key_grad_out, out_sems.at[2 * ROWS + 1])

    @pl.loop(0, ROWS)
    def _(block):
        grad_block(
            block, first + block, random_ref, global_ref, queries, grads, values, key_turned,
            value_turned, shared_ref, picked_ref, dpicked_ref, inverse_ref, window_ref,
            global_sum_ref, attended_ref, query_grad_ref,
        )
        for copy in block_out(block):
            copy.start()
        for k in range(2):

            @pl.when((block == k + 2) & edge)
            def _(k=k):
                value_scatter.edge_hop(k)

    def between(k):
        if k == 0:

            @pl.when(inner)
            def _():
                value_scatter.inner_hop(0)

        if k == 2:

            @pl.when(edge)
            def _():
                value_scatter.edge_hop(2)

            @pl.when(inner)
            def _():
                value_scatter.inner_hop(1)

    owners(key_scatter, 1.0 / math.sqrt(HD), dpicked_ref, queries, between)

    @pl.when(edge)
    def _():
        key_scatter.edge_hop(0)
        key_scatter.edge_hop(1)
        value_scatter.edge_finish(value_grad_ref)
        key_scatter.edge_hop(2)
        key_scatter.edge_finish(key_grad_ref)

    @pl.when(inner)
    def _():
        value_scatter.inner_hop(2)
        value_scatter.inner_finish(value_grad_ref)
        for k in range(LINE - 1):
            key_scatter.inner_hop(k)
        key_scatter.inner_finish(key_grad_ref)

    value_out.start()
    key_out.start()
    key_gather.wait_sends()
    value_gather.wait_sends()
    value_scatter.wait_sends()
    key_scatter.wait_sends()
    for block in range(ROWS):
        for copy in block_out(block):
            copy.wait()
    value_out.wait()
    key_out.wait()


def deliver_kernel(*refs):
    count = (len(refs) - 1) // 3
    sources, targets, held, sems = refs[:count], refs[count : 2 * count], refs[2 * count : -1], refs[-1]
    loads = [
        pltpu.make_async_copy(sources[i], held[i], sems.at[i]) for i in range(count)
    ]
    stores = [
        pltpu.make_async_copy(held[i], targets[i], sems.at[count + i]) for i in range(count)
    ]
    for load in loads:
        load.start()
    for load, store in zip(loads, stores):
        load.wait()
        store.start()
    for store in stores:
        store.wait()


def deliver(*arrays):
    count = len(arrays)
    return pl.pallas_call(
        deliver_kernel,
        in_specs=[pl.BlockSpec(memory_space=pltpu.HBM)] * count,
        out_specs=[pl.BlockSpec(memory_space=pltpu.HBM)] * count,
        out_shape=[jax.ShapeDtypeStruct(a.shape, a.dtype) for a in arrays],
        scratch_shapes=[pltpu.VMEM(a.shape, a.dtype) for a in arrays]
        + [pltpu.SemaphoreType.DMA((2 * count,))],
        compiler_params=pltpu.CompilerParams(vmem_limit_bytes=FUSED_MIB * 1024 * 1024),
        name="deliver",
    )(*arrays)


def fused_call(random_ids, global_ids, segments, queries, out_grads, keys, values):
    smem = pl.BlockSpec(memory_space=pltpu.SMEM)
    hbm = pl.BlockSpec(memory_space=pltpu.HBM)
    half = jnp.bfloat16
    wide = jnp.float32
    total_blocks = SEQ * ROWS
    dma = pltpu.SemaphoreType.DMA

    def tiles(*count, kind=half):
        return pltpu.VMEM(count + (BLK, HD), kind)

    gather_sems = [
        dma((count * HALVES,)) for count in (5, LINE, LINE, LINE, 2 * LINE, 2 * LINE)
    ]
    scatter_parts = [
        tiles(2 * LINE, ROWS, kind=wide),
        tiles(2 * LINE, ROWS),
        tiles(2 * LINE, ROWS),
        tiles(LINE, ROWS),
        tiles(LINE, ROWS),
        tiles(LINE - 1, ROWS),
        tiles(5, ROWS),
    ] + [dma((count,)) for count in (2 * LINE, 2 * LINE, LINE * HALVES, LINE * HALVES, 3 * HALVES, 5 * HALVES)]
    return pl.pallas_call(
        fused_kernel,
        in_specs=[smem, smem, hbm, hbm, hbm, hbm, hbm],
        out_specs=[hbm] * 4,
        out_shape=[
            jax.ShapeDtypeStruct((ROWS, BLK, HQ * HD), half),
            jax.ShapeDtypeStruct((ROWS, BLK, HQ * HD), half),
            jax.ShapeDtypeStruct(keys.shape, half),
            jax.ShapeDtypeStruct(keys.shape, half),
        ],
        scratch_shapes=[
            tiles(total_blocks),
            tiles(total_blocks),
            tiles(total_blocks),
            tiles(total_blocks),
            tiles(ROWS, HQ),
            tiles(ROWS, HQ),
            tiles(total_blocks + 1),
            pltpu.VMEM((ROWS, 5, BLK, HQ * BLK), half),
            tiles(PICKS),
            tiles(PICKS),
            pltpu.VMEM((ROWS, 8, HQ * BLK), wide),
            tiles(ROWS + 2, kind=wide),
            tiles(G + 2, kind=wide),
            tiles(EACH + 1, kind=wide),
            tiles(ROWS, kind=wide),
            pltpu.VMEM((8, BLK), jnp.int32),
            pltpu.SMEM((8, BLK), jnp.int32),
            pltpu.VMEM((total_blocks, BLK), jnp.int32),
            pltpu.VMEM((ROWS, BLK, HQ * HD), half),
            pltpu.VMEM((ROWS, BLK, HQ * HD), half),
            tiles(ROWS),
            tiles(ROWS),
            dma((4 + 2 * HQ,)),
            dma((2 * ROWS + 2,)),
        ]
        + gather_sems * 2
        + scatter_parts * 2,
        compiler_params=pltpu.CompilerParams(
            collective_id=0, has_side_effects=True, vmem_limit_bytes=FUSED_MIB * 1024 * 1024
        ),
        name="fused_attention",
    )(random_ids, global_ids, segments, queries, out_grads, keys, values)


FUSED_MIB = 60


def fused_body(queries, key_rows, value_rows, out_grads, segment_ids, random_blocks, global_blocks):
    total_blocks = segment_ids.shape[0] // BLK

    def blocks(array):
        return array.reshape(ROWS, BLK, -1)

    attended, query_grads, key_grads, value_grads = fused_call(
        random_blocks.transpose(2, 0, 1),
        global_blocks,
        segment_ids.reshape(total_blocks, BLK),
        blocks(queries),
        blocks(out_grads),
        blocks(key_rows),
        blocks(value_rows),
    )
    tokens = ROWS * BLK
    return deliver(
        attended.reshape(tokens, -1),
        query_grads.reshape(tokens, -1),
        key_grads.reshape(tokens, -1),
        value_grads.reshape(tokens, -1),
    )


def plan(*arrays):
    tokens = arrays[4].shape[0]
    fits = tokens * 2 * HD * 4 <= DENSE_BYTES
    chosen = fused_body if fits and arrays[0].shape[0] == ROWS * BLK and lax.axis_size("seq") == SEQ else body
    return chosen(*arrays)


def solution(mesh):
    placed = (
        P(("shard", "seq"), None),
        P(("shard", "seq"), None),
        P(("shard", "seq"), None),
        P(("shard", "seq"), None),
        P("shard"),
        P(("shard", "seq"), None, None),
        P("shard"),
    )
    return jax.shard_map(
        plan,
        mesh=mesh,
        in_specs=placed,
        out_specs=(
            P(("shard", "seq"), None),
            P(("shard", "seq"), None),
            P(("shard", "seq"), None),
            P(("shard", "seq"), None),
        ),
        check_vma=False,
    )
```

```python
import math

import jax
import jax.numpy as jnp
from jax import lax
from jax.experimental import pallas as pl
from jax.experimental.pallas import tpu as pltpu
from jax.sharding import PartitionSpec as P

HD = 128
HQ = 8
BLK = 128
RAND = 3
G = 2


masked_value = -1e30


def with_halo(array, sides, width):
    for axis, dim in sides:
        size, length = (lax.axis_size(axis), array.shape[dim])
        up = [(i, (i + 1) % size) for i in range(size - 1)]
        down = [(j, i) for i, j in up]
        last = lax.slice_in_dim(array, length - width, length, axis=dim)
        first = lax.slice_in_dim(array, 0, width, axis=dim)
        before = lax.ppermute(last, axis, up)
        after = lax.ppermute(first, axis, down)
        array = jnp.concatenate([before, array, after], axis=dim)
    return array


def spread(block, axis, owner):
    block = jnp.where(lax.axis_index(axis) == owner, block, jnp.zeros_like(block))
    return lax.psum(block, axis)


def from_behind(block, axis, distance):
    devices = range(lax.axis_size(axis))
    route = [(i - distance, i) for i in devices if i - distance in devices]
    return lax.ppermute(block, axis, route)


def routing(block_ids, per_device):
    owners = block_ids // per_device
    ordering = jnp.arange(block_ids.shape[0])
    earlier = (owners[:, None] == owners[None, :]) & (ordering[None, :] < ordering[:, None])
    return (owners, jnp.sum(earlier.astype(jnp.int32), axis=1))


def taken(blocks, indices):
    return lax.map(lambda i: lax.dynamic_index_in_dim(blocks, i, 0, keepdims=False), indices)


def block_pass(
    query_block,
    grad_block,
    shared,
    shared_live,
    query_segs,
    shared_segs,
    random_kv,
    random_segs,
    scaling,
):
    wide = jnp.float32
    shared_mask = (query_segs[:, None, None] == shared_segs[None]) & shared_live[None, :, None]
    random_mask = query_segs[None, :, None, None] == random_segs[:, None]
    shared_scores = (
        jnp.einsum("thd,jkd->htjk", query_block, shared[:, :, :HD], preferred_element_type=wide)
        * scaling
    )
    shared_scores = jnp.where(shared_mask[None], shared_scores, masked_value)
    random_scores = (
        jnp.einsum(
            "thd,hrkd->htrk", query_block, random_kv[:, :, :, :HD], preferred_element_type=wide
        )
        * scaling
    )
    random_scores = jnp.where(random_mask, random_scores, masked_value)
    top_score = jnp.maximum(
        jnp.max(shared_scores, axis=(2, 3)), jnp.max(random_scores, axis=(2, 3))
    )
    totals = jnp.sum(jnp.exp(shared_scores - top_score[:, :, None, None]), axis=(2, 3))
    totals = totals + jnp.sum(jnp.exp(random_scores - top_score[:, :, None, None]), axis=(2, 3))
    log_totals = top_score + jnp.log(totals)
    shared_probs = jnp.exp(shared_scores - log_totals[:, :, None, None])
    random_probs = jnp.exp(random_scores - log_totals[:, :, None, None])
    shared_half = shared_probs.astype(jnp.bfloat16)
    random_half = random_probs.astype(jnp.bfloat16)
    attended = jnp.einsum(
        "htjk,jkd->thd", shared_half, shared[:, :, HD:], preferred_element_type=wide
    )
    attended = attended + jnp.einsum(
        "htrk,hrkd->thd", random_half, random_kv[:, :, :, HD:], preferred_element_type=wide
    )
    attended = attended.astype(jnp.bfloat16)
    row_dots = jnp.einsum("thd,thd->ht", grad_block, attended, preferred_element_type=wide)
    shared_dprobs = jnp.einsum(
        "thd,jkd->htjk", grad_block, shared[:, :, HD:], preferred_element_type=wide
    )
    random_dprobs = jnp.einsum(
        "thd,hrkd->htrk", grad_block, random_kv[:, :, :, HD:], preferred_element_type=wide
    )
    shared_dscores = (shared_probs * (shared_dprobs - row_dots[:, :, None, None])).astype(
        jnp.bfloat16
    )
    random_dscores = (random_probs * (random_dprobs - row_dots[:, :, None, None])).astype(
        jnp.bfloat16
    )
    query_grads = jnp.einsum(
        "htjk,jkd->thd", shared_dscores, shared[:, :, :HD], preferred_element_type=wide
    )
    query_grads = query_grads + jnp.einsum(
        "htrk,hrkd->thd", random_dscores, random_kv[:, :, :, :HD], preferred_element_type=wide
    )
    query_grads = (query_grads * scaling).astype(jnp.bfloat16)
    shared_kgrad = (
        jnp.einsum("htjk,thd->jkd", shared_dscores, query_block, preferred_element_type=wide)
        * scaling
    )
    shared_vgrad = jnp.einsum("htjk,thd->jkd", shared_half, grad_block, preferred_element_type=wide)
    shared_grads = jnp.where(
        shared_live[:, None, None], jnp.concatenate([shared_kgrad, shared_vgrad], axis=2), 0.0
    )
    random_kgrad = (
        jnp.einsum("htrk,thd->hrkd", random_dscores, query_block, preferred_element_type=wide)
        * scaling
    )
    random_vgrad = jnp.einsum(
        "htrk,thd->hrkd", random_half, grad_block, preferred_element_type=wide
    )
    random_grads = jnp.concatenate([random_kgrad, random_vgrad], axis=3)
    return (attended, query_grads, shared_grads, random_grads, log_totals, row_dots)


def body(queries, key_rows, value_rows, out_grads, segment_ids, random_blocks, global_blocks):
    scaling = 1.0 / math.sqrt(HD)
    row_count = queries.shape[0]
    qcount = row_count // BLK
    devices = lax.axis_size("seq")
    position = lax.axis_index("seq")
    total_blocks = segment_ids.shape[0] // BLK
    seg_blocks = segment_ids.reshape(total_blocks, BLK)
    joined = jnp.concatenate([key_rows, value_rows], axis=1)
    local_blocks = joined.reshape(qcount, BLK, 2 * HD)
    padded = with_halo(joined, (("seq", 0),), BLK)
    owned = global_blocks // qcount == position
    pieces = []
    for global_slot in range(G):
        picked = lax.dynamic_index_in_dim(
            local_blocks, global_blocks[global_slot] % qcount, 0, keepdims=False
        )
        pieces.append(spread(picked, "seq", global_blocks[global_slot] // qcount))
    global_kv = jnp.stack(pieces)
    chosen_ids = random_blocks.reshape(-1)
    pick_count = chosen_ids.shape[0]
    capacity = -(-pick_count // devices)
    owners, slots = routing(chosen_ids, qcount)
    outgoing_ids = (
        jnp.full((devices, capacity), -1, jnp.int32).at[owners, slots].set(chosen_ids % qcount)
    )
    wanted = lax.all_to_all(outgoing_ids, "seq", split_axis=0, concat_axis=0, tiled=True)
    wanted_clip = jnp.clip(wanted, 0, qcount - 1)
    served = taken(local_blocks, wanted_clip.reshape(-1)).reshape(wanted.shape + (BLK, 2 * HD))
    answer = lax.all_to_all(served, "seq", split_axis=0, concat_axis=0, tiled=True)
    answer = answer.reshape(devices * capacity, BLK, 2 * HD)
    random_kv = taken(answer, owners * capacity + slots)
    random_kv = random_kv.reshape(qcount, HQ, RAND, BLK, 2 * HD)
    query_blocks = queries.reshape(qcount, BLK, HQ, HD)
    grad_blocks = out_grads.reshape(qcount, BLK, HQ, HD)

    def attend(bundle):
        block_index, query_block, grad_block, block_kv, block_ids = bundle
        global_index = position * qcount + block_index
        window = lax.dynamic_slice_in_dim(padded, block_index * BLK, 3 * BLK, 0).reshape(
            3, BLK, 2 * HD
        )
        window_ids = global_index + jnp.arange(-1, 2, dtype=jnp.int32)
        window_live = (window_ids >= 0) & (window_ids < total_blocks)
        shared_ids = jnp.concatenate([jnp.clip(window_ids, 0, total_blocks - 1), global_blocks])
        shared_live = jnp.concatenate([window_live, jnp.ones((G,), bool)])
        shared = jnp.concatenate([window, global_kv], axis=0)
        return block_pass(
            query_block,
            grad_block,
            shared,
            shared_live,
            seg_blocks[global_index],
            seg_blocks[shared_ids],
            block_kv,
            seg_blocks[block_ids],
            scaling,
        )

    attended, query_grads, shared_grads, random_grads, log_totals, row_dots = lax.map(
        attend,
        (jnp.arange(qcount, dtype=jnp.int32), query_blocks, grad_blocks, random_kv, random_blocks),
    )
    window_sum = jnp.zeros((qcount + 2, BLK, 2 * HD), jnp.float32)
    for offset in range(3):
        window_sum = window_sum.at[offset : offset + qcount].add(shared_grads[:, offset])
    from_right = from_behind(window_sum[0].astype(jnp.bfloat16), "seq", -1).astype(jnp.float32)
    from_left = from_behind(window_sum[qcount + 1].astype(jnp.bfloat16), "seq", 1).astype(
        jnp.float32
    )
    own_grads = window_sum[1 : qcount + 1]
    own_grads = own_grads.at[qcount - 1].add(from_right).at[0].add(from_left)
    global_sum = lax.psum(jnp.sum(shared_grads[:, 3:], axis=0), "seq")
    global_hits = (
        (global_blocks[:, None] % qcount == jnp.arange(qcount)[None, :]) & owned[:, None]
    ).astype(jnp.float32)
    own_grads = own_grads + jnp.einsum(
        "gq,gkd->qkd", global_hits, global_sum, precision=lax.Precision.HIGHEST
    )
    outgoing = (
        jnp.zeros((devices, capacity, BLK, 2 * HD), jnp.float32)
        .at[owners, slots]
        .set(random_grads.reshape(pick_count, BLK, 2 * HD))
    )
    returned = lax.all_to_all(outgoing, "seq", split_axis=0, concat_axis=0, tiled=True)
    request_hits = (wanted[:, :, None] == jnp.arange(qcount)[None, None, :]).astype(jnp.float32)
    own_grads = own_grads + jnp.einsum(
        "ncq,nckd->qkd", request_hits, returned, precision=lax.Precision.HIGHEST
    )
    own_flat = own_grads.reshape(row_count, 2 * HD)
    return (
        attended.reshape(row_count, HQ * HD),
        query_grads.reshape(row_count, HQ * HD),
        own_flat[:, :HD].astype(jnp.bfloat16),
        own_flat[:, HD:].astype(jnp.bfloat16),
    )


LOG2E = 1.4426950408889634
DENSE_BYTES = 16 * 1024 * 1024
LINE = 4
SEQ = 16


class Place:
    def __init__(self):
        me = lax.axis_index("seq")
        self.me = me
        self.core = lax.rem(me, 2)
        self.x = lax.rem(me // 2, 2)
        self.z = me // 4
        self.high = self.z // 2
        self.step = 1 - 2 * self.high
        self.inner = jnp.where((self.z == 1) | (self.z == 2), 1, 0)
        self.partner = self.at(self.z, self.x, 1 - self.core)
        self.across = self.at(self.z, 1 - self.x, self.core)
        self.onward = self.at(self.z + self.step, self.x, self.core)
        self.outward = self.at(self.z - self.step, self.x, self.core)

    def at(self, z, x, core):
        return z * 4 + x * 2 + core


def greet(place):
    barrier = pltpu.get_barrier_semaphore()
    for other in (place.partner, place.across, place.onward):
        pl.semaphore_signal(
            barrier, inc=1, device_id={"seq": other}, device_id_type=pl.DeviceIdType.MESH
        )

    @pl.when(place.inner == 1)
    def _():
        pl.semaphore_signal(
            barrier, inc=1, device_id={"seq": place.outward}, device_id_type=pl.DeviceIdType.MESH
        )

    pl.semaphore_wait(barrier, 3 + place.inner)


def remote(source, target, send, receive, device):
    return pltpu.make_async_remote_copy(
        src_ref=source,
        dst_ref=target,
        send_sem=send,
        recv_sem=receive,
        device_id={"seq": device},
        device_id_type=pl.DeviceIdType.MESH,
    )


ROWS = 4
PICKS = ROWS * HQ * RAND
EACH = PICKS // SEQ
HALVES = 2


class Gather:
    def __init__(self, place, buffer, zs, zr, xs, xr, cs, cr):
        self.place = place
        z, step, inner = place.z, place.step, place.inner
        lines = [z, z + step - 2 * step * inner, z + step * (2 - inner), z + step * (3 - inner)]
        self.own = [place.at(line, place.x, place.core) for line in lines]
        self.other = [place.at(line, 1 - place.x, place.core) for line in lines]
        self.own_far = [place.at(line, place.x, 1 - place.core) for line in lines]
        self.other_far = [place.at(line, 1 - place.x, 1 - place.core) for line in lines]
        width = ROWS // HALVES

        def copies(owner, sends, at, receives, to, device):
            made = []
            for half in range(HALVES):
                part = buffer.at[pl.ds(owner * ROWS + half * width, width)]
                made.append(
                    remote(
                        part,
                        part,
                        sends.at[at * HALVES + half],
                        receives.at[to * HALVES + half],
                        device,
                    )
                )
            return made

        onward, outward = place.onward, place.outward
        own, other = self.own, self.other
        self.edge = copies(own[0], zs, 0, zr, 1, onward)
        self.along = copies(own[0], zs, 0, zr, 2, onward)
        self.out = copies(own[0], zs, 1, zr, 1, outward)
        self.relays = [
            copies(own[1], zs, 2, zr, 3, onward),
            copies(own[2], zs, 3, zr, 2, outward),
            copies(own[3], zs, 4, zr, 3, outward),
        ]
        self.arrivals = [copies(own[k], zs, 0, zr, k, onward) for k in range(LINE)]
        self.crossing = [copies(own[k], xs, k, xr, k, place.across) for k in range(LINE)]
        self.crossed = [copies(other[k], xs, k, xr, k, place.across) for k in range(LINE)]
        self.near = [copies(own[k], cs, k, cr, k, place.partner) for k in range(LINE)]
        self.far = [copies(other[k], cs, LINE + k, cr, LINE + k, place.partner) for k in range(LINE)]

    def start_line(self):
        @pl.when(self.place.inner == 0)
        def _():
            for copy in self.edge:
                copy.start()

        @pl.when(self.place.inner == 1)
        def _():
            for half in range(HALVES):
                self.out[half].start()
                self.along[half].start()

    def start_cross(self):
        for half in range(HALVES):
            self.crossing[0][half].start()
            self.near[0][half].start()

    def line_arrival(self, k, cross=True):
        for half in range(HALVES):
            self.arrivals[k][half].wait_recv()

            @pl.when(self.place.inner == 1)
            def _(half=half):
                self.relays[k - 1][half].start()

            if cross:
                self.crossing[k][half].start()
            self.near[k][half].start()

    def cross_late(self, k):
        for half in range(HALVES):
            self.crossing[k][half].start()

    def cross_arrival(self, k):
        for half in range(HALVES):
            self.crossed[k][half].wait_recv()
            self.far[k][half].start()

    def near_arrival(self, k):
        for half in range(HALVES):
            self.near[k][half].wait_recv()

    def far_arrival(self, k):
        for half in range(HALVES):
            self.far[k][half].wait_recv()

    def wait_sends(self):
        for half in range(HALVES):
            self.edge[half].wait_send()
            for k in range(LINE):
                self.crossing[k][half].wait_send()
                self.near[k][half].wait_send()
                self.far[k][half].wait_send()

        @pl.when(self.place.inner == 1)
        def _():
            for half in range(HALVES):
                self.out[half].wait_send()
                for relay in self.relays:
                    relay[half].wait_send()


class Scatter:
    def __init__(
        self, place, kept, pair_out, pair_in, cross_out, cross_in, line_out, line_in,
        ps, pr, xs, xr, zs, zr,
    ):
        self.place = place
        self.kept, self.pair_out, self.pair_in = kept, pair_out, pair_in
        self.cross_out, self.cross_in = cross_out, cross_in
        self.line_out, self.line_in = line_out, line_in
        self.sems = (ps, pr, xs, xr, zs, zr)
        z, high = place.z, place.high
        self.order = [3 * (1 - high), 2 - high, 1 - z + 4 * high, z]

    def pair(self, index):
        ps, pr = self.sems[:2]
        return remote(
            self.pair_out.at[index], self.pair_in.at[index], ps.at[index], pr.at[index],
            self.place.partner,
        )

    def cross(self, k, half):
        xs, xr = self.sems[2:4]
        at = k * HALVES + half
        return remote(
            self.cross_out.at[k, part(half)], self.cross_in.at[k, part(half)], xs.at[at],
            xr.at[at], self.place.across,
        )

    def hop(self, k, slot, half, device):
        zs, zr = self.sems[4:]
        return remote(
            self.line_out.at[k, part(half)], self.line_in.at[slot, part(half)],
            zs.at[k * HALVES + half], zr.at[slot * HALVES + half], device,
        )

    def start_cross(self, k):
        self.pair(2 * k).wait_recv()
        for half in range(HALVES):
            total = self.kept[2 * k, part(half)] + self.pair_in[2 * k, part(half)].astype(jnp.float32)
            self.cross_out[k, part(half)] = total.astype(jnp.bfloat16)
            self.cross(k, half).start()

    def local(self, k, half):
        wide = jnp.float32
        self.cross(k, half).wait_recv()
        total = self.kept[2 * k + 1, part(half)] + self.pair_in[2 * k + 1, part(half)].astype(wide)
        return total + self.cross_in[k, part(half)].astype(wide)

    def arrived(self, slot, half):
        self.hop(0, slot, half, self.place.onward).wait_recv()
        return self.line_in[slot, part(half)].astype(jnp.float32)

    def edge_hop(self, k):
        self.pair(2 * k + 1).wait_recv()
        for half in range(HALVES):
            self.line_out[k, part(half)] = self.local(k, half).astype(jnp.bfloat16)
            self.hop(k, k, half, self.place.onward).start()

    def inner_hop(self, k):
        self.pair(2 * k + 1).wait_recv()
        for half in range(HALVES):
            total = self.local(k, half) + self.arrived(k if k < 2 else 3, half)
            self.line_out[k, part(half)] = total.astype(jnp.bfloat16)
            if k < 2:
                self.hop(k, 3 + k, half, self.place.onward).start()
            else:
                self.hop(k, 0, half, self.place.outward).start()

    def finish(self, result, slots):
        k = LINE - 1
        self.pair(2 * k + 1).wait_recv()
        for half in range(HALVES):
            total = self.local(k, half)
            for slot in slots:
                total = total + self.arrived(slot, half)
            result[part(half)] = total.astype(result.dtype)

    def edge_finish(self, result):
        self.finish(result, (0,))

    def inner_finish(self, result):
        self.finish(result, (2, 4))

    def wait_sends(self):
        for index in range(2 * LINE):
            self.pair(index).wait_send()
        for half in range(HALVES):
            for k in range(LINE):
                self.cross(k, half).wait_send()
            for k in range(LINE - 1):
                self.hop(k, k, half, self.place.onward).wait_send()


def part(half):
    return pl.ds(half * (ROWS // HALVES), ROWS // HALVES)


def pick_table(random_ref, table_ref):
    shape = (BLK, BLK)
    lane = lax.broadcasted_iota(jnp.int32, shape, 1)
    row = lax.broadcasted_iota(jnp.int32, shape, 0)
    far = 1 << 20
    by_lane = jnp.full((8, BLK), far, jnp.int32)
    small = lax.broadcasted_iota(jnp.int32, (8, BLK), 1)
    by_row = jnp.full(shape, far, jnp.int32)
    for pick in range(PICKS):
        name = random_ref[pick % RAND, pick // (HQ * RAND), pick // RAND % HQ]
        by_lane = jnp.where(small == pick, name * BLK, by_lane)
        by_row = jnp.where(row == pick, name * BLK, by_row)
    by_lane = by_lane + small
    by_row = by_row + row
    rank = jnp.sum((by_lane[0:1] < by_row).astype(jnp.int32), axis=1, keepdims=True)
    code = row * 64 + ((row * 171) >> 9)
    ordered = jnp.sum(jnp.where(rank == lane, code, 0), axis=0, keepdims=True)
    before = jnp.sum((by_row < lane * BLK).astype(jnp.int32), axis=0, keepdims=True)
    table_ref[0:1] = ordered
    table_ref[1:2] = before


def against(rows, columns):
    return lax.dot_general(
        rows, columns, (((1,), (1,)), ((), ())), preferred_element_type=jnp.float32
    )


def product(rows, columns):
    return jnp.dot(rows, columns, preferred_element_type=jnp.float32)


def names_of(mine, block, random_ref, global_ref, total_blocks):
    shared_ids = [
        jnp.maximum(mine - 1, 0),
        mine,
        jnp.minimum(mine + 1, total_blocks - 1),
        global_ref[0],
        global_ref[1],
    ]
    random_ids = [[random_ref[pick, block, head] for pick in range(RAND)] for head in range(HQ)]
    return shared_ids, random_ids


def add_shared(block, tiles, stack, window_ref, global_sum_ref):
    sums = product(jnp.concatenate(tiles[:5], axis=0), stack)
    for slot in range(3):
        window_ref[block + slot] += sums[span(slot)]
    for slot in range(G):
        global_sum_ref[1 + slot] += sums[span(3 + slot)]


def span(head):
    return slice(head * BLK, (head + 1) * BLK)


def key_flags(boundary, name):
    shape = (BLK, HD)
    row = lax.broadcasted_iota(jnp.int32, shape, 0)
    lane = lax.broadcasted_iota(jnp.int32, shape, 1)
    low = row < boundary - name * BLK
    one = jnp.where((lane == 0) & low, 1.0, 0.0) + jnp.where(lane == 1, 1.0, 0.0)
    return (one - jnp.where((lane == 1) & low, 1.0, 0.0)).astype(jnp.bfloat16)


def query_flags(boundary, name):
    shape = (BLK, HD)
    row = lax.broadcasted_iota(jnp.int32, shape, 0)
    lane = lax.broadcasted_iota(jnp.int32, shape, 1)
    low = row < boundary - name * BLK
    one = jnp.where((lane == 1) & low, masked_value, 0.0)
    two = jnp.where(lane == 0, masked_value, 0.0) - jnp.where((lane == 0) & low, masked_value, 0.0)
    return (one + two).astype(jnp.bfloat16)


def split(shared, picked):
    tiles = [shared[span(slot)] for slot in range(5)]
    for pick in range(RAND):
        tiles.append(jnp.concatenate([part[span(pick)] for part in picked], axis=1))
    return tiles


def score_block(
    block, mine, boundary, random_ref, global_ref, query_ref, grad_ref, key_ref, flag_ref,
    shared_ref, picked_ref, inverse_ref, window_ref, global_sum_ref,
):
    half = jnp.bfloat16
    total_blocks = key_ref.shape[0]
    shared_ids, random_ids = names_of(mine, block, random_ref, global_ref, total_blocks)
    flag_ids = list(shared_ids)
    flag_ids[0] = jnp.where(mine == 0, total_blocks, flag_ids[0])
    flag_ids[2] = jnp.where(mine == total_blocks - 1, total_blocks, flag_ids[2])

    def flagged(ids, flag_ids):
        return jnp.concatenate(
            [jnp.concatenate([key_ref[i], flag_ref[j]], axis=1) for i, j in zip(ids, flag_ids)],
            axis=0,
        )

    mark = query_flags(boundary, mine)
    factor = LOG2E / math.sqrt(HD)
    marked = [jnp.concatenate([query_ref[block, head], mark], axis=1) for head in range(HQ)]
    stack = jnp.concatenate(marked, axis=0)
    shared = against(flagged(shared_ids, flag_ids), stack)
    picked = [
        against(flagged(random_ids[head], random_ids[head]), marked[head]) for head in range(HQ)
    ]
    scores = split(shared, picked)
    top = scores[0]
    for tile in scores[1:]:
        top = jnp.maximum(top, tile)
    top = jnp.max(top, axis=0, keepdims=True) * factor
    powers = [jnp.exp2(tile * factor - top) for tile in scores]
    total = powers[0]
    for tile in powers[1:]:
        total = total + tile
    inverse = 1.0 / jnp.sum(total, axis=0, keepdims=True)
    powers = [tile.astype(half) for tile in powers]
    for slot in range(5):
        shared_ref[block, slot] = powers[slot]
    for pick in range(RAND):
        for head in range(HQ):
            picked_ref[(block * HQ + head) * RAND + pick] = powers[5 + pick][:, span(head)]
    inverse_ref[block, 0:1] = inverse
    scaled = []
    for head in range(HQ):
        turned = jnp.broadcast_to(inverse[:, span(head)], (BLK, BLK)).T
        scaled.append((grad_ref[block, head].astype(jnp.float32) * turned).astype(half))
        grad_ref[block, head] = scaled[head]
    add_shared(block, powers, jnp.concatenate(scaled, axis=0), window_ref, global_sum_ref)


def entries(source, shared_ids, random_ids, parts):
    def stacked(ids):
        return jnp.concatenate([source[i] for i in ids], axis=0)

    shared = against(stacked(shared_ids), jnp.concatenate(parts, axis=0))
    return split(shared, [against(stacked(random_ids[head]), parts[head]) for head in range(HQ)])


def gathered(turned, shared_ids, random_ids, tiles):
    shared = product(
        jnp.concatenate([turned[i] for i in shared_ids], axis=1),
        jnp.concatenate(tiles[:5], axis=0),
    )
    pieces = []
    for head in range(HQ):
        pieces.append(
            product(
                jnp.concatenate([turned[i] for i in random_ids[head]], axis=1),
                jnp.concatenate([tile[:, span(head)] for tile in tiles[5:]], axis=0),
            )
        )
    return shared + jnp.concatenate(pieces, axis=1)


def grad_block(
    block, mine, random_ref, global_ref, query_ref, grad_ref, value_ref, key_turned, value_turned,
    shared_ref, picked_ref, dpicked_ref, inverse_ref, window_ref, global_sum_ref,
    attended_ref, query_grad_ref,
):
    wide = jnp.float32
    half = jnp.bfloat16
    total_blocks = value_ref.shape[0]
    shared_ids, random_ids = names_of(mine, block, random_ref, global_ref, total_blocks)
    queries = [query_ref[block, head] for head in range(HQ)]
    grads = [grad_ref[block, head] for head in range(HQ)]
    probs = [shared_ref[block, slot] for slot in range(5)]
    for pick in range(RAND):
        probs.append(
            jnp.concatenate(
                [picked_ref[(block * HQ + head) * RAND + pick] for head in range(HQ)], axis=1
            )
        )
    attended = gathered(value_turned, shared_ids, random_ids, probs) * inverse_ref[block, 0:1]
    attended = attended.astype(half).astype(wide)
    grads_turned = jnp.concatenate([part.astype(wide).T for part in grads], axis=1)
    row_dots = jnp.sum(attended * grads_turned, axis=0, keepdims=True)
    for head in range(HQ):
        attended_ref[block, :, span(head)] = attended[:, span(head)].T.astype(half)
    dprobs = entries(value_ref, shared_ids, random_ids, grads)
    dscores = [(p.astype(wide) * (d - row_dots)).astype(half) for p, d in zip(probs, dprobs)]
    for pick in range(RAND):
        for head in range(HQ):
            dpicked_ref[(block * HQ + head) * RAND + pick] = dscores[5 + pick][:, span(head)]
    add_shared(block, dscores, jnp.concatenate(queries, axis=0), window_ref, global_sum_ref)
    query_grads = gathered(key_turned, shared_ids, random_ids, dscores) * (1.0 / math.sqrt(HD))
    for head in range(HQ):
        query_grad_ref[block, :, span(head)] = query_grads[:, span(head)].T.astype(half)


def sum_owner(
    index, scatter, scale, table, global_ref, tiles_ref, rows_ref, window_ref, global_sum_ref,
    running_ref, owner_ref,
):
    place = scatter.place
    side, k, kind = index // (2 * LINE), lax.rem(index // 2, LINE), lax.rem(index, 2)
    line = scatter.order[3]
    for other in (2, 1, 0):
        line = jnp.where(k == other, scatter.order[other], line)
    x = jnp.where(side == 0, 1 - place.x, place.x)
    core = jnp.where(kind == 0, 1 - place.core, place.core)
    owner = place.at(line, x, core)
    running = None
    for pick in range(EACH):
        code = table[0, owner * EACH + pick]
        term = product(tiles_ref[code >> 6], rows_ref[(code >> 3) & 7, code & 7])
        running = term if running is None else running + term
        running_ref[pick + 1] = running
    for row in range(ROWS):
        name = owner * ROWS + row
        first = jnp.clip(table[1, name] - owner * EACH, 0, EACH)
        last = jnp.clip(table[1, name + 1] - owner * EACH, 0, EACH)
        hit = jnp.where(global_ref[0] == name, 1, 0) + jnp.where(global_ref[1] == name, 2, 0)
        owner_ref[row] = running_ref[last] - running_ref[first] + global_sum_ref[hit]

    @pl.when(owner == place.me)
    def _():
        for row in range(ROWS):
            owner_ref[row] += window_ref[1 + row]

    @pl.when(owner == place.me - 1)
    def _():
        owner_ref[ROWS - 1] += window_ref[0]

    @pl.when(owner == place.me + 1)
    def _():
        owner_ref[0] += window_ref[ROWS + 1]

    slot = 2 * k + side

    @pl.when(kind == 0)
    def _():
        scatter.pair_out[slot] = (owner_ref[...] * scale).astype(jnp.bfloat16)
        scatter.pair(slot).start()

    @pl.when(kind == 1)
    def _():
        scatter.kept[slot] = owner_ref[...] * scale


def fused_kernel(
    random_ref, global_ref, segment_in, query_in, grad_in, key_in, value_in,
    attended_out, query_grad_out, key_grad_out, value_grad_out,
    keys, values, key_turned, value_turned, queries, grads, flag_ref, shared_ref, picked_ref,
    dpicked_ref, inverse_ref, window_ref, global_sum_ref, running_ref, owner_ref, table_vec, table, segment_ref,
    attended_ref, query_grad_ref, key_grad_ref, value_grad_ref, local_sems, out_sems,
    *rest,
):
    place = Place()
    wide = jnp.float32
    total_blocks = keys.shape[0]
    key_sems, value_sems, rest = rest[:6], rest[6:12], rest[12:]
    value_scatter = Scatter(place, *rest[:13])
    key_scatter = Scatter(place, *rest[13:])
    me = place.me
    first = me * ROWS
    own = pl.ds(first, ROWS)
    loads = [
        pltpu.make_async_copy(key_in, keys.at[own], local_sems.at[0]),
        pltpu.make_async_copy(value_in, values.at[own], local_sems.at[1]),
        pltpu.make_async_copy(segment_in, segment_ref, local_sems.at[3 + 2 * HQ]),
    ]
    for head in range(HQ):
        span = pl.ds(head * HD, HD)
        loads.append(
            pltpu.make_async_copy(
                query_in.at[:, :, span], queries.at[:, head], local_sems.at[2 + head]
            )
        )
        loads.append(
            pltpu.make_async_copy(
                grad_in.at[:, :, span], grads.at[:, head], local_sems.at[2 + HQ + head]
            )
        )
    for load in loads[:3]:
        load.start()
    greet(place)
    for load in loads[:3]:
        load.wait()
    key_gather = Gather(place, keys, *key_sems)
    value_gather = Gather(place, values, *value_sems)

    def turn(source, target, owner):
        for row in range(ROWS):
            target[owner * ROWS + row] = source[owner * ROWS + row].T

    def turn_keys(owner):
        turn(keys, key_turned, owner)

    def turn_values(owner):
        turn(values, value_turned, owner)

    key_gather.start_line()
    value_gather.start_line()
    key_gather.start_cross()
    value_gather.start_cross()
    for load in loads[3:]:
        load.start()
    pick_table(random_ref, table_vec)
    table_copy = pltpu.make_async_copy(table_vec, table, local_sems.at[2 + 2 * HQ])
    table_copy.start()
    zero = jnp.zeros((BLK, HD), wide)

    def clear():
        for row in range(ROWS + 2):
            window_ref[row] = zero
        for slot in range(G + 2):
            global_sum_ref[slot] = zero

    clear()
    running_ref[0] = zero
    boundary = jnp.sum((segment_ref[...] == segment_ref[0:1, 0:1]).astype(jnp.int32))
    @pl.loop(0, total_blocks)
    def _(name):
        flag_ref[name] = key_flags(boundary, name)

    flag_ref[total_blocks] = jnp.where(
        lax.broadcasted_iota(jnp.int32, (BLK, HD), 1) < 2, 1.0, 0.0
    ).astype(jnp.bfloat16)
    key_gather.line_arrival(1)
    key_gather.cross_arrival(0)
    turn_keys(key_gather.own[0])
    turn_values(key_gather.own[0])
    key_gather.line_arrival(2)
    value_gather.cross_arrival(0)
    turn_keys(key_gather.own[1])
    turn_keys(key_gather.other[0])
    key_gather.cross_arrival(1)
    value_gather.line_arrival(1, cross=False)
    turn_values(value_gather.own[1])
    turn_values(value_gather.other[0])
    key_gather.line_arrival(3)
    value_gather.cross_late(1)
    turn_keys(key_gather.own[2])
    turn_keys(key_gather.other[1])
    value_gather.line_arrival(2)
    turn_keys(key_gather.own[3])
    turn_values(value_gather.own[2])
    key_gather.cross_arrival(2)
    turn_keys(key_gather.other[2])
    value_gather.line_arrival(3)
    turn_values(value_gather.own[3])
    for k in range(LINE - 1):
        key_gather.near_arrival(k)
        turn_keys(key_gather.own_far[k])
        key_gather.far_arrival(k)
        turn_keys(key_gather.other_far[k])
        value_gather.near_arrival(k)
        turn_values(value_gather.own_far[k])
    value_gather.far_arrival(0)
    turn_values(value_gather.other_far[0])
    key_gather.cross_arrival(3)
    key_gather.near_arrival(3)
    for load in loads[3:]:
        load.wait()
    table_copy.wait()
    key_gather.far_arrival(3)

    @pl.loop(0, ROWS)
    def _(block):
        score_block(
            block, first + block, boundary, random_ref, global_ref, queries, grads, keys,
            flag_ref, shared_ref, picked_ref, inverse_ref, window_ref, global_sum_ref,
        )
        for k in range(1, LINE):

            @pl.when(block == k - 1)
            def _(k=k):
                value_gather.cross_arrival(k)

    def owners(scatter, scale, tiles_ref, rows_ref, events):
        global_sum_ref[3] = global_sum_ref[1] + global_sum_ref[2]

        @pl.loop(0, SEQ)
        def _(index):
            sum_owner(
                index, scatter, scale, table, global_ref, tiles_ref, rows_ref, window_ref,
                global_sum_ref, running_ref, owner_ref,
            )
            for k in range(LINE):

                @pl.when(index == 2 * k + 6)
                def _(k=k):
                    scatter.start_cross(k)

            events(index)

    owners(value_scatter, 1.0, picked_ref, grads, lambda index: None)
    clear()
    value_gather.near_arrival(3)
    turn_values(value_gather.own_far[3])
    turn_keys(key_gather.other[3])
    turn_keys(key_gather.own_far[3])
    turn_keys(key_gather.other_far[3])
    for k in range(1, LINE):
        turn_values(value_gather.other[k])
        value_gather.far_arrival(k)
        turn_values(value_gather.other_far[k])
    edge, inner = place.inner == 0, place.inner == 1

    def block_out(block):
        return [
            pltpu.make_async_copy(source.at[block], target.at[block], out_sems.at[at * ROWS + block])
            for at, (source, target) in enumerate(
                [(attended_ref, attended_out), (query_grad_ref, query_grad_out)]
            )
        ]

    value_out = pltpu.make_async_copy(value_grad_ref, value_grad_out, out_sems.at[2 * ROWS])
    key_out = pltpu.make_async_copy(key_grad_ref, key_grad_out, out_sems.at[2 * ROWS + 1])

    @pl.loop(0, ROWS)
    def _(block):
        grad_block(
            block, first + block, random_ref, global_ref, queries, grads, values, key_turned,
            value_turned, shared_ref, picked_ref, dpicked_ref, inverse_ref, window_ref,
            global_sum_ref, attended_ref, query_grad_ref,
        )
        for copy in block_out(block):
            copy.start()
        for k in range(3):

            @pl.when((block == k + 1) & edge)
            def _(k=k):
                value_scatter.edge_hop(k)

        @pl.when((block == 3) & inner)
        def _():
            value_scatter.inner_hop(0)

    def between(index):
        for k in (1, 2):

            @pl.when((index == 4 * k + 7) & inner)
            def _(k=k):
                value_scatter.inner_hop(k)

    owners(key_scatter, 1.0 / math.sqrt(HD), dpicked_ref, queries, between)

    @pl.when(edge)
    def _():
        key_scatter.edge_hop(0)
        key_scatter.edge_hop(1)
        value_scatter.edge_finish(value_grad_ref)
        key_scatter.edge_hop(2)
        key_scatter.edge_finish(key_grad_ref)

    @pl.when(inner)
    def _():
        value_scatter.inner_finish(value_grad_ref)
        for k in range(LINE - 1):
            key_scatter.inner_hop(k)
        key_scatter.inner_finish(key_grad_ref)

    value_out.start()
    key_out.start()
    key_gather.wait_sends()
    value_gather.wait_sends()
    value_scatter.wait_sends()
    key_scatter.wait_sends()
    for block in range(ROWS):
        for copy in block_out(block):
            copy.wait()
    value_out.wait()
    key_out.wait()


def deliver_kernel(*refs):
    count = (len(refs) - 1) // 3
    sources, targets, held, sems = refs[:count], refs[count : 2 * count], refs[2 * count : -1], refs[-1]
    loads = [
        pltpu.make_async_copy(sources[i], held[i], sems.at[i]) for i in range(count)
    ]
    stores = [
        pltpu.make_async_copy(held[i], targets[i], sems.at[count + i]) for i in range(count)
    ]
    for load in loads:
        load.start()
    for load, store in zip(loads, stores):
        load.wait()
        store.start()
    for store in stores:
        store.wait()


def deliver(*arrays):
    count = len(arrays)
    return pl.pallas_call(
        deliver_kernel,
        in_specs=[pl.BlockSpec(memory_space=pltpu.HBM)] * count,
        out_specs=[pl.BlockSpec(memory_space=pltpu.HBM)] * count,
        out_shape=[jax.ShapeDtypeStruct(a.shape, a.dtype) for a in arrays],
        scratch_shapes=[pltpu.VMEM(a.shape, a.dtype) for a in arrays]
        + [pltpu.SemaphoreType.DMA((2 * count,))],
        compiler_params=pltpu.CompilerParams(vmem_limit_bytes=FUSED_MIB * 1024 * 1024),
        name="deliver",
    )(*arrays)


def fused_call(random_ids, global_ids, segments, queries, out_grads, keys, values):
    smem = pl.BlockSpec(memory_space=pltpu.SMEM)
    hbm = pl.BlockSpec(memory_space=pltpu.HBM)
    half = jnp.bfloat16
    wide = jnp.float32
    total_blocks = SEQ * ROWS
    dma = pltpu.SemaphoreType.DMA

    def tiles(*count, kind=half):
        return pltpu.VMEM(count + (BLK, HD), kind)

    gather_sems = [
        dma((count * HALVES,)) for count in (5, LINE, LINE, LINE, 2 * LINE, 2 * LINE)
    ]
    scatter_parts = [
        tiles(2 * LINE, ROWS, kind=wide),
        tiles(2 * LINE, ROWS),
        tiles(2 * LINE, ROWS),
        tiles(LINE, ROWS),
        tiles(LINE, ROWS),
        tiles(LINE - 1, ROWS),
        tiles(5, ROWS),
    ] + [dma((count,)) for count in (2 * LINE, 2 * LINE, LINE * HALVES, LINE * HALVES, 3 * HALVES, 5 * HALVES)]
    return pl.pallas_call(
        fused_kernel,
        in_specs=[smem, smem, hbm, hbm, hbm, hbm, hbm],
        out_specs=[hbm] * 4,
        out_shape=[
            jax.ShapeDtypeStruct((ROWS, BLK, HQ * HD), half),
            jax.ShapeDtypeStruct((ROWS, BLK, HQ * HD), half),
            jax.ShapeDtypeStruct(keys.shape, half),
            jax.ShapeDtypeStruct(keys.shape, half),
        ],
        scratch_shapes=[
            tiles(total_blocks),
            tiles(total_blocks),
            tiles(total_blocks),
            tiles(total_blocks),
            tiles(ROWS, HQ),
            tiles(ROWS, HQ),
            tiles(total_blocks + 1),
            pltpu.VMEM((ROWS, 5, BLK, HQ * BLK), half),
            tiles(PICKS),
            tiles(PICKS),
            pltpu.VMEM((ROWS, 8, HQ * BLK), wide),
            tiles(ROWS + 2, kind=wide),
            tiles(G + 2, kind=wide),
            tiles(EACH + 1, kind=wide),
            tiles(ROWS, kind=wide),
            pltpu.VMEM((8, BLK), jnp.int32),
            pltpu.SMEM((8, BLK), jnp.int32),
            pltpu.VMEM((total_blocks, BLK), jnp.int32),
            pltpu.VMEM((ROWS, BLK, HQ * HD), half),
            pltpu.VMEM((ROWS, BLK, HQ * HD), half),
            tiles(ROWS),
            tiles(ROWS),
            dma((4 + 2 * HQ,)),
            dma((2 * ROWS + 2,)),
        ]
        + gather_sems * 2
        + scatter_parts * 2,
        compiler_params=pltpu.CompilerParams(
            collective_id=0, has_side_effects=True, vmem_limit_bytes=FUSED_MIB * 1024 * 1024
        ),
        name="fused_attention",
    )(random_ids, global_ids, segments, queries, out_grads, keys, values)


FUSED_MIB = 60


def fused_body(queries, key_rows, value_rows, out_grads, segment_ids, random_blocks, global_blocks):
    total_blocks = segment_ids.shape[0] // BLK

    def blocks(array):
        return array.reshape(ROWS, BLK, -1)

    attended, query_grads, key_grads, value_grads = fused_call(
        random_blocks.transpose(2, 0, 1),
        global_blocks,
        segment_ids.reshape(total_blocks, BLK),
        blocks(queries),
        blocks(out_grads),
        blocks(key_rows),
        blocks(value_rows),
    )
    tokens = ROWS * BLK
    return deliver(
        attended.reshape(tokens, -1),
        query_grads.reshape(tokens, -1),
        key_grads.reshape(tokens, -1),
        value_grads.reshape(tokens, -1),
    )


def plan(*arrays):
    tokens = arrays[4].shape[0]
    fits = tokens * 2 * HD * 4 <= DENSE_BYTES
    chosen = fused_body if fits and arrays[0].shape[0] == ROWS * BLK and lax.axis_size("seq") == SEQ else body
    return chosen(*arrays)


def solution(mesh):
    placed = (
        P(("shard", "seq"), None),
        P(("shard", "seq"), None),
        P(("shard", "seq"), None),
        P(("shard", "seq"), None),
        P("shard"),
        P(("shard", "seq"), None, None),
        P("shard"),
    )
    return jax.shard_map(
        plan,
        mesh=mesh,
        in_specs=placed,
        out_specs=(
            P(("shard", "seq"), None),
            P(("shard", "seq"), None),
            P(("shard", "seq"), None),
            P(("shard", "seq"), None),
        ),
        check_vma=False,
    )
```

```python
import math

import jax
import jax.numpy as jnp
from jax import lax
from jax.experimental import pallas as pl
from jax.experimental.pallas import tpu as pltpu
from jax.sharding import PartitionSpec as P

HD = 128
HQ = 8
BLK = 128
RAND = 3
G = 2


masked_value = -1e30


def with_halo(array, sides, width):
    for axis, dim in sides:
        size, length = (lax.axis_size(axis), array.shape[dim])
        up = [(i, (i + 1) % size) for i in range(size - 1)]
        down = [(j, i) for i, j in up]
        last = lax.slice_in_dim(array, length - width, length, axis=dim)
        first = lax.slice_in_dim(array, 0, width, axis=dim)
        before = lax.ppermute(last, axis, up)
        after = lax.ppermute(first, axis, down)
        array = jnp.concatenate([before, array, after], axis=dim)
    return array


def spread(block, axis, owner):
    block = jnp.where(lax.axis_index(axis) == owner, block, jnp.zeros_like(block))
    return lax.psum(block, axis)


def from_behind(block, axis, distance):
    devices = range(lax.axis_size(axis))
    route = [(i - distance, i) for i in devices if i - distance in devices]
    return lax.ppermute(block, axis, route)


def routing(block_ids, per_device):
    owners = block_ids // per_device
    ordering = jnp.arange(block_ids.shape[0])
    earlier = (owners[:, None] == owners[None, :]) & (ordering[None, :] < ordering[:, None])
    return (owners, jnp.sum(earlier.astype(jnp.int32), axis=1))


def taken(blocks, indices):
    return lax.map(lambda i: lax.dynamic_index_in_dim(blocks, i, 0, keepdims=False), indices)


def block_pass(
    query_block,
    grad_block,
    shared,
    shared_live,
    query_segs,
    shared_segs,
    random_kv,
    random_segs,
    scaling,
):
    wide = jnp.float32
    shared_mask = (query_segs[:, None, None] == shared_segs[None]) & shared_live[None, :, None]
    random_mask = query_segs[None, :, None, None] == random_segs[:, None]
    shared_scores = (
        jnp.einsum("thd,jkd->htjk", query_block, shared[:, :, :HD], preferred_element_type=wide)
        * scaling
    )
    shared_scores = jnp.where(shared_mask[None], shared_scores, masked_value)
    random_scores = (
        jnp.einsum(
            "thd,hrkd->htrk", query_block, random_kv[:, :, :, :HD], preferred_element_type=wide
        )
        * scaling
    )
    random_scores = jnp.where(random_mask, random_scores, masked_value)
    top_score = jnp.maximum(
        jnp.max(shared_scores, axis=(2, 3)), jnp.max(random_scores, axis=(2, 3))
    )
    totals = jnp.sum(jnp.exp(shared_scores - top_score[:, :, None, None]), axis=(2, 3))
    totals = totals + jnp.sum(jnp.exp(random_scores - top_score[:, :, None, None]), axis=(2, 3))
    log_totals = top_score + jnp.log(totals)
    shared_probs = jnp.exp(shared_scores - log_totals[:, :, None, None])
    random_probs = jnp.exp(random_scores - log_totals[:, :, None, None])
    shared_half = shared_probs.astype(jnp.bfloat16)
    random_half = random_probs.astype(jnp.bfloat16)
    attended = jnp.einsum(
        "htjk,jkd->thd", shared_half, shared[:, :, HD:], preferred_element_type=wide
    )
    attended = attended + jnp.einsum(
        "htrk,hrkd->thd", random_half, random_kv[:, :, :, HD:], preferred_element_type=wide
    )
    attended = attended.astype(jnp.bfloat16)
    row_dots = jnp.einsum("thd,thd->ht", grad_block, attended, preferred_element_type=wide)
    shared_dprobs = jnp.einsum(
        "thd,jkd->htjk", grad_block, shared[:, :, HD:], preferred_element_type=wide
    )
    random_dprobs = jnp.einsum(
        "thd,hrkd->htrk", grad_block, random_kv[:, :, :, HD:], preferred_element_type=wide
    )
    shared_dscores = (shared_probs * (shared_dprobs - row_dots[:, :, None, None])).astype(
        jnp.bfloat16
    )
    random_dscores = (random_probs * (random_dprobs - row_dots[:, :, None, None])).astype(
        jnp.bfloat16
    )
    query_grads = jnp.einsum(
        "htjk,jkd->thd", shared_dscores, shared[:, :, :HD], preferred_element_type=wide
    )
    query_grads = query_grads + jnp.einsum(
        "htrk,hrkd->thd", random_dscores, random_kv[:, :, :, :HD], preferred_element_type=wide
    )
    query_grads = (query_grads * scaling).astype(jnp.bfloat16)
    shared_kgrad = (
        jnp.einsum("htjk,thd->jkd", shared_dscores, query_block, preferred_element_type=wide)
        * scaling
    )
    shared_vgrad = jnp.einsum("htjk,thd->jkd", shared_half, grad_block, preferred_element_type=wide)
    shared_grads = jnp.where(
        shared_live[:, None, None], jnp.concatenate([shared_kgrad, shared_vgrad], axis=2), 0.0
    )
    random_kgrad = (
        jnp.einsum("htrk,thd->hrkd", random_dscores, query_block, preferred_element_type=wide)
        * scaling
    )
    random_vgrad = jnp.einsum(
        "htrk,thd->hrkd", random_half, grad_block, preferred_element_type=wide
    )
    random_grads = jnp.concatenate([random_kgrad, random_vgrad], axis=3)
    return (attended, query_grads, shared_grads, random_grads, log_totals, row_dots)


def body(queries, key_rows, value_rows, out_grads, segment_ids, random_blocks, global_blocks):
    scaling = 1.0 / math.sqrt(HD)
    row_count = queries.shape[0]
    qcount = row_count // BLK
    devices = lax.axis_size("seq")
    position = lax.axis_index("seq")
    total_blocks = segment_ids.shape[0] // BLK
    seg_blocks = segment_ids.reshape(total_blocks, BLK)
    joined = jnp.concatenate([key_rows, value_rows], axis=1)
    local_blocks = joined.reshape(qcount, BLK, 2 * HD)
    padded = with_halo(joined, (("seq", 0),), BLK)
    owned = global_blocks // qcount == position
    pieces = []
    for global_slot in range(G):
        picked = lax.dynamic_index_in_dim(
            local_blocks, global_blocks[global_slot] % qcount, 0, keepdims=False
        )
        pieces.append(spread(picked, "seq", global_blocks[global_slot] // qcount))
    global_kv = jnp.stack(pieces)
    chosen_ids = random_blocks.reshape(-1)
    pick_count = chosen_ids.shape[0]
    capacity = -(-pick_count // devices)
    owners, slots = routing(chosen_ids, qcount)
    outgoing_ids = (
        jnp.full((devices, capacity), -1, jnp.int32).at[owners, slots].set(chosen_ids % qcount)
    )
    wanted = lax.all_to_all(outgoing_ids, "seq", split_axis=0, concat_axis=0, tiled=True)
    wanted_clip = jnp.clip(wanted, 0, qcount - 1)
    served = taken(local_blocks, wanted_clip.reshape(-1)).reshape(wanted.shape + (BLK, 2 * HD))
    answer = lax.all_to_all(served, "seq", split_axis=0, concat_axis=0, tiled=True)
    answer = answer.reshape(devices * capacity, BLK, 2 * HD)
    random_kv = taken(answer, owners * capacity + slots)
    random_kv = random_kv.reshape(qcount, HQ, RAND, BLK, 2 * HD)
    query_blocks = queries.reshape(qcount, BLK, HQ, HD)
    grad_blocks = out_grads.reshape(qcount, BLK, HQ, HD)

    def attend(bundle):
        block_index, query_block, grad_block, block_kv, block_ids = bundle
        global_index = position * qcount + block_index
        window = lax.dynamic_slice_in_dim(padded, block_index * BLK, 3 * BLK, 0).reshape(
            3, BLK, 2 * HD
        )
        window_ids = global_index + jnp.arange(-1, 2, dtype=jnp.int32)
        window_live = (window_ids >= 0) & (window_ids < total_blocks)
        shared_ids = jnp.concatenate([jnp.clip(window_ids, 0, total_blocks - 1), global_blocks])
        shared_live = jnp.concatenate([window_live, jnp.ones((G,), bool)])
        shared = jnp.concatenate([window, global_kv], axis=0)
        return block_pass(
            query_block,
            grad_block,
            shared,
            shared_live,
            seg_blocks[global_index],
            seg_blocks[shared_ids],
            block_kv,
            seg_blocks[block_ids],
            scaling,
        )

    attended, query_grads, shared_grads, random_grads, log_totals, row_dots = lax.map(
        attend,
        (jnp.arange(qcount, dtype=jnp.int32), query_blocks, grad_blocks, random_kv, random_blocks),
    )
    window_sum = jnp.zeros((qcount + 2, BLK, 2 * HD), jnp.float32)
    for offset in range(3):
        window_sum = window_sum.at[offset : offset + qcount].add(shared_grads[:, offset])
    from_right = from_behind(window_sum[0].astype(jnp.bfloat16), "seq", -1).astype(jnp.float32)
    from_left = from_behind(window_sum[qcount + 1].astype(jnp.bfloat16), "seq", 1).astype(
        jnp.float32
    )
    own_grads = window_sum[1 : qcount + 1]
    own_grads = own_grads.at[qcount - 1].add(from_right).at[0].add(from_left)
    global_sum = lax.psum(jnp.sum(shared_grads[:, 3:], axis=0), "seq")
    global_hits = (
        (global_blocks[:, None] % qcount == jnp.arange(qcount)[None, :]) & owned[:, None]
    ).astype(jnp.float32)
    own_grads = own_grads + jnp.einsum(
        "gq,gkd->qkd", global_hits, global_sum, precision=lax.Precision.HIGHEST
    )
    outgoing = (
        jnp.zeros((devices, capacity, BLK, 2 * HD), jnp.float32)
        .at[owners, slots]
        .set(random_grads.reshape(pick_count, BLK, 2 * HD))
    )
    returned = lax.all_to_all(outgoing, "seq", split_axis=0, concat_axis=0, tiled=True)
    request_hits = (wanted[:, :, None] == jnp.arange(qcount)[None, None, :]).astype(jnp.float32)
    own_grads = own_grads + jnp.einsum(
        "ncq,nckd->qkd", request_hits, returned, precision=lax.Precision.HIGHEST
    )
    own_flat = own_grads.reshape(row_count, 2 * HD)
    return (
        attended.reshape(row_count, HQ * HD),
        query_grads.reshape(row_count, HQ * HD),
        own_flat[:, :HD].astype(jnp.bfloat16),
        own_flat[:, HD:].astype(jnp.bfloat16),
    )


LOG2E = 1.4426950408889634
DENSE_BYTES = 16 * 1024 * 1024
LINE = 4
SEQ = 16


class Place:
    def __init__(self):
        me = lax.axis_index("seq")
        self.me = me
        self.core = lax.rem(me, 2)
        self.x = lax.rem(me // 2, 2)
        self.z = me // 4
        self.high = self.z // 2
        self.step = 1 - 2 * self.high
        self.inner = jnp.where((self.z == 1) | (self.z == 2), 1, 0)
        self.partner = self.at(self.z, self.x, 1 - self.core)
        self.across = self.at(self.z, 1 - self.x, self.core)
        self.onward = self.at(self.z + self.step, self.x, self.core)
        self.outward = self.at(self.z - self.step, self.x, self.core)

    def at(self, z, x, core):
        return z * 4 + x * 2 + core


def greet(place):
    barrier = pltpu.get_barrier_semaphore()
    for other in (place.partner, place.across, place.onward):
        pl.semaphore_signal(
            barrier, inc=1, device_id={"seq": other}, device_id_type=pl.DeviceIdType.MESH
        )

    @pl.when(place.inner == 1)
    def _():
        pl.semaphore_signal(
            barrier, inc=1, device_id={"seq": place.outward}, device_id_type=pl.DeviceIdType.MESH
        )

    pl.semaphore_wait(barrier, 3 + place.inner)


def remote(source, target, send, receive, device):
    return pltpu.make_async_remote_copy(
        src_ref=source,
        dst_ref=target,
        send_sem=send,
        recv_sem=receive,
        device_id={"seq": device},
        device_id_type=pl.DeviceIdType.MESH,
    )


ROWS = 4
PICKS = ROWS * HQ * RAND
EACH = PICKS // SEQ
HALVES = 2


class Gather:
    def __init__(self, place, buffer, zs, zr, xs, xr, cs, cr):
        self.place = place
        z, step, inner = place.z, place.step, place.inner
        lines = [z, z + step - 2 * step * inner, z + step * (2 - inner), z + step * (3 - inner)]
        self.own = [place.at(line, place.x, place.core) for line in lines]
        self.other = [place.at(line, 1 - place.x, place.core) for line in lines]
        self.own_far = [place.at(line, place.x, 1 - place.core) for line in lines]
        self.other_far = [place.at(line, 1 - place.x, 1 - place.core) for line in lines]
        width = ROWS // HALVES

        def copies(owner, sends, at, receives, to, device):
            made = []
            for half in range(HALVES):
                part = buffer.at[pl.ds(owner * ROWS + half * width, width)]
                made.append(
                    remote(
                        part,
                        part,
                        sends.at[at * HALVES + half],
                        receives.at[to * HALVES + half],
                        device,
                    )
                )
            return made

        onward, outward = place.onward, place.outward
        own, other = self.own, self.other
        self.edge = copies(own[0], zs, 0, zr, 1, onward)
        self.along = copies(own[0], zs, 0, zr, 2, onward)
        self.out = copies(own[0], zs, 1, zr, 1, outward)
        self.relays = [
            copies(own[1], zs, 2, zr, 3, onward),
            copies(own[2], zs, 3, zr, 2, outward),
            copies(own[3], zs, 4, zr, 3, outward),
        ]
        self.arrivals = [copies(own[k], zs, 0, zr, k, onward) for k in range(LINE)]
        self.crossing = [copies(own[k], xs, k, xr, k, place.across) for k in range(LINE)]
        self.crossed = [copies(other[k], xs, k, xr, k, place.across) for k in range(LINE)]
        self.near = [copies(own[k], cs, k, cr, k, place.partner) for k in range(LINE)]
        self.far = [copies(other[k], cs, LINE + k, cr, LINE + k, place.partner) for k in range(LINE)]

    def start_line(self):
        @pl.when(self.place.inner == 0)
        def _():
            for copy in self.edge:
                copy.start()

        @pl.when(self.place.inner == 1)
        def _():
            for half in range(HALVES):
                self.out[half].start()
                self.along[half].start()

    def start_cross(self):
        for half in range(HALVES):
            self.crossing[0][half].start()
            self.near[0][half].start()

    def line_arrival(self, k, cross=True):
        for half in range(HALVES):
            self.arrivals[k][half].wait_recv()

            @pl.when(self.place.inner == 1)
            def _(half=half):
                self.relays[k - 1][half].start()

            if cross:
                self.crossing[k][half].start()
            self.near[k][half].start()

    def cross_late(self, k):
        for half in range(HALVES):
            self.crossing[k][half].start()

    def cross_arrival(self, k):
        for half in range(HALVES):
            self.crossed[k][half].wait_recv()
            self.far[k][half].start()

    def near_arrival(self, k):
        for half in range(HALVES):
            self.near[k][half].wait_recv()

    def far_arrival(self, k):
        for half in range(HALVES):
            self.far[k][half].wait_recv()

    def wait_sends(self):
        for half in range(HALVES):
            self.edge[half].wait_send()
            for k in range(LINE):
                self.crossing[k][half].wait_send()
                self.near[k][half].wait_send()
                self.far[k][half].wait_send()

        @pl.when(self.place.inner == 1)
        def _():
            for half in range(HALVES):
                self.out[half].wait_send()
                for relay in self.relays:
                    relay[half].wait_send()


class Scatter:
    def __init__(
        self, place, kept, pair_out, pair_in, cross_out, cross_in, line_out, line_in,
        ps, pr, xs, xr, zs, zr,
    ):
        self.place = place
        self.kept, self.pair_out, self.pair_in = kept, pair_out, pair_in
        self.cross_out, self.cross_in = cross_out, cross_in
        self.line_out, self.line_in = line_out, line_in
        self.sems = (ps, pr, xs, xr, zs, zr)
        z, high = place.z, place.high
        self.order = [3 * (1 - high), 2 - high, 1 - z + 4 * high, z]

    def pair(self, index):
        ps, pr = self.sems[:2]
        return remote(
            self.pair_out.at[index], self.pair_in.at[index], ps.at[index], pr.at[index],
            self.place.partner,
        )

    def cross(self, k, half):
        xs, xr = self.sems[2:4]
        at = k * HALVES + half
        return remote(
            self.cross_out.at[k, part(half)], self.cross_in.at[k, part(half)], xs.at[at],
            xr.at[at], self.place.across,
        )

    def hop(self, k, slot, half, device):
        zs, zr = self.sems[4:]
        return remote(
            self.line_out.at[k, part(half)], self.line_in.at[slot, part(half)],
            zs.at[k * HALVES + half], zr.at[slot * HALVES + half], device,
        )

    def start_cross(self, k):
        self.pair(2 * k).wait_recv()
        for half in range(HALVES):
            total = self.kept[2 * k, part(half)] + self.pair_in[2 * k, part(half)].astype(jnp.float32)
            self.cross_out[k, part(half)] = total.astype(jnp.bfloat16)
            self.cross(k, half).start()

    def local(self, k, half):
        wide = jnp.float32
        self.cross(k, half).wait_recv()
        total = self.kept[2 * k + 1, part(half)] + self.pair_in[2 * k + 1, part(half)].astype(wide)
        return total + self.cross_in[k, part(half)].astype(wide)

    def arrived(self, slot, half):
        self.hop(0, slot, half, self.place.onward).wait_recv()
        return self.line_in[slot, part(half)].astype(jnp.float32)

    def edge_hop(self, k):
        self.pair(2 * k + 1).wait_recv()
        for half in range(HALVES):
            self.line_out[k, part(half)] = self.local(k, half).astype(jnp.bfloat16)
            self.hop(k, k, half, self.place.onward).start()

    def inner_hop(self, k):
        self.pair(2 * k + 1).wait_recv()
        for half in range(HALVES):
            total = self.local(k, half) + self.arrived(k if k < 2 else 3, half)
            self.line_out[k, part(half)] = total.astype(jnp.bfloat16)
            if k < 2:
                self.hop(k, 3 + k, half, self.place.onward).start()
            else:
                self.hop(k, 0, half, self.place.outward).start()

    def finish(self, result, slots):
        k = LINE - 1
        self.pair(2 * k + 1).wait_recv()
        for half in range(HALVES):
            total = self.local(k, half)
            for slot in slots:
                total = total + self.arrived(slot, half)
            result[part(half)] = total.astype(result.dtype)

    def edge_finish(self, result):
        self.finish(result, (0,))

    def inner_finish(self, result):
        self.finish(result, (2, 4))

    def wait_sends(self):
        for index in range(2 * LINE):
            self.pair(index).wait_send()
        for half in range(HALVES):
            for k in range(LINE):
                self.cross(k, half).wait_send()
            for k in range(LINE - 1):
                self.hop(k, k, half, self.place.onward).wait_send()


def part(half):
    return pl.ds(half * (ROWS // HALVES), ROWS // HALVES)


def pick_table(random_ref, table_ref):
    shape = (BLK, BLK)
    lane = lax.broadcasted_iota(jnp.int32, shape, 1)
    row = lax.broadcasted_iota(jnp.int32, shape, 0)
    far = 1 << 20
    by_lane = jnp.full((8, BLK), far, jnp.int32)
    small = lax.broadcasted_iota(jnp.int32, (8, BLK), 1)
    by_row = jnp.full(shape, far, jnp.int32)
    for pick in range(PICKS):
        name = random_ref[pick % RAND, pick // (HQ * RAND), pick // RAND % HQ]
        by_lane = jnp.where(small == pick, name * BLK, by_lane)
        by_row = jnp.where(row == pick, name * BLK, by_row)
    by_lane = by_lane + small
    by_row = by_row + row
    rank = jnp.sum((by_lane[0:1] < by_row).astype(jnp.int32), axis=1, keepdims=True)
    code = row * 64 + ((row * 171) >> 9)
    ordered = jnp.sum(jnp.where(rank == lane, code, 0), axis=0, keepdims=True)
    before = jnp.sum((by_row < lane * BLK).astype(jnp.int32), axis=0, keepdims=True)
    table_ref[0:1] = ordered
    table_ref[1:2] = before


def against(rows, columns):
    return lax.dot_general(
        rows, columns, (((1,), (1,)), ((), ())), preferred_element_type=jnp.float32
    )


def product(rows, columns):
    return jnp.dot(rows, columns, preferred_element_type=jnp.float32)


def names_of(mine, block, random_ref, global_ref, total_blocks):
    shared_ids = [
        jnp.maximum(mine - 1, 0),
        mine,
        jnp.minimum(mine + 1, total_blocks - 1),
        global_ref[0],
        global_ref[1],
    ]
    random_ids = [[random_ref[pick, block, head] for pick in range(RAND)] for head in range(HQ)]
    return shared_ids, random_ids


def add_shared(block, tiles, stack, window_ref, global_sum_ref):
    sums = product(jnp.concatenate(tiles[:5], axis=0), stack)
    for slot in range(3):
        window_ref[block + slot] += sums[span(slot)]
    for slot in range(G):
        global_sum_ref[1 + slot] += sums[span(3 + slot)]


def span(head):
    return slice(head * BLK, (head + 1) * BLK)


def key_flags(boundary, name):
    shape = (BLK, HD)
    row = lax.broadcasted_iota(jnp.int32, shape, 0)
    lane = lax.broadcasted_iota(jnp.int32, shape, 1)
    low = row < boundary - name * BLK
    one = jnp.where((lane == 0) & low, 1.0, 0.0) + jnp.where(lane == 1, 1.0, 0.0)
    return (one - jnp.where((lane == 1) & low, 1.0, 0.0)).astype(jnp.bfloat16)


def query_flags(boundary, name):
    shape = (BLK, HD)
    row = lax.broadcasted_iota(jnp.int32, shape, 0)
    lane = lax.broadcasted_iota(jnp.int32, shape, 1)
    low = row < boundary - name * BLK
    one = jnp.where((lane == 1) & low, masked_value, 0.0)
    two = jnp.where(lane == 0, masked_value, 0.0) - jnp.where((lane == 0) & low, masked_value, 0.0)
    return (one + two).astype(jnp.bfloat16)


def split(shared, picked):
    tiles = [shared[span(slot)] for slot in range(5)]
    for pick in range(RAND):
        tiles.append(jnp.concatenate([part[span(pick)] for part in picked], axis=1))
    return tiles


def score_block(
    block, mine, boundary, random_ref, global_ref, query_ref, grad_ref, key_ref, flag_ref,
    shared_ref, picked_ref, inverse_ref, window_ref, global_sum_ref,
):
    half = jnp.bfloat16
    total_blocks = key_ref.shape[0]
    shared_ids, random_ids = names_of(mine, block, random_ref, global_ref, total_blocks)
    flag_ids = list(shared_ids)
    flag_ids[0] = jnp.where(mine == 0, total_blocks, flag_ids[0])
    flag_ids[2] = jnp.where(mine == total_blocks - 1, total_blocks, flag_ids[2])

    def flagged(ids, flag_ids):
        return jnp.concatenate(
            [jnp.concatenate([key_ref[i], flag_ref[j]], axis=1) for i, j in zip(ids, flag_ids)],
            axis=0,
        )

    mark = query_flags(boundary, mine)
    factor = LOG2E / math.sqrt(HD)
    marked = [jnp.concatenate([query_ref[block, head], mark], axis=1) for head in range(HQ)]
    stack = jnp.concatenate(marked, axis=0)
    shared = against(flagged(shared_ids, flag_ids), stack)
    picked = [
        against(flagged(random_ids[head], random_ids[head]), marked[head]) for head in range(HQ)
    ]
    scores = split(shared, picked)
    top = scores[0]
    for tile in scores[1:]:
        top = jnp.maximum(top, tile)
    top = jnp.max(top, axis=0, keepdims=True) * factor
    powers = [jnp.exp2(tile * factor - top) for tile in scores]
    total = powers[0]
    for tile in powers[1:]:
        total = total + tile
    inverse = 1.0 / jnp.sum(total, axis=0, keepdims=True)
    powers = [tile.astype(half) for tile in powers]
    for slot in range(5):
        shared_ref[block, slot] = powers[slot]
    for pick in range(RAND):
        for head in range(HQ):
            picked_ref[(block * HQ + head) * RAND + pick] = powers[5 + pick][:, span(head)]
    inverse_ref[block, 0:1] = inverse
    scaled = []
    for head in range(HQ):
        turned = jnp.broadcast_to(inverse[:, span(head)], (BLK, BLK)).T
        scaled.append((grad_ref[block, head].astype(jnp.float32) * turned).astype(half))
        grad_ref[block, head] = scaled[head]
    add_shared(block, powers, jnp.concatenate(scaled, axis=0), window_ref, global_sum_ref)


def entries(source, shared_ids, random_ids, parts):
    def stacked(ids):
        return jnp.concatenate([source[i] for i in ids], axis=0)

    shared = against(stacked(shared_ids), jnp.concatenate(parts, axis=0))
    return split(shared, [against(stacked(random_ids[head]), parts[head]) for head in range(HQ)])


def gathered(turned, shared_ids, random_ids, tiles):
    shared = product(
        jnp.concatenate([turned[i] for i in shared_ids], axis=1),
        jnp.concatenate(tiles[:5], axis=0),
    )
    pieces = []
    for head in range(HQ):
        pieces.append(
            product(
                jnp.concatenate([turned[i] for i in random_ids[head]], axis=1),
                jnp.concatenate([tile[:, span(head)] for tile in tiles[5:]], axis=0),
            )
        )
    return shared + jnp.concatenate(pieces, axis=1)


def grad_block(
    block, mine, random_ref, global_ref, query_ref, grad_ref, value_ref, key_turned, value_turned,
    shared_ref, picked_ref, dpicked_ref, inverse_ref, window_ref, global_sum_ref,
    attended_ref, query_grad_ref,
):
    wide = jnp.float32
    half = jnp.bfloat16
    total_blocks = value_ref.shape[0]
    shared_ids, random_ids = names_of(mine, block, random_ref, global_ref, total_blocks)
    queries = [query_ref[block, head] for head in range(HQ)]
    grads = [grad_ref[block, head] for head in range(HQ)]
    probs = [shared_ref[block, slot] for slot in range(5)]
    for pick in range(RAND):
        probs.append(
            jnp.concatenate(
                [picked_ref[(block * HQ + head) * RAND + pick] for head in range(HQ)], axis=1
            )
        )
    attended = gathered(value_turned, shared_ids, random_ids, probs) * inverse_ref[block, 0:1]
    attended = attended.astype(half).astype(wide)
    grads_turned = jnp.concatenate([part.astype(wide).T for part in grads], axis=1)
    row_dots = jnp.sum(attended * grads_turned, axis=0, keepdims=True)
    for head in range(HQ):
        attended_ref[block, :, span(head)] = attended[:, span(head)].T.astype(half)
    dprobs = entries(value_ref, shared_ids, random_ids, grads)
    dscores = [(p.astype(wide) * (d - row_dots)).astype(half) for p, d in zip(probs, dprobs)]
    for pick in range(RAND):
        for head in range(HQ):
            dpicked_ref[(block * HQ + head) * RAND + pick] = dscores[5 + pick][:, span(head)]
    add_shared(block, dscores, jnp.concatenate(queries, axis=0), window_ref, global_sum_ref)
    query_grads = gathered(key_turned, shared_ids, random_ids, dscores) * (1.0 / math.sqrt(HD))
    for head in range(HQ):
        query_grad_ref[block, :, span(head)] = query_grads[:, span(head)].T.astype(half)


def sum_owner(
    index, scatter, scale, table, global_ref, tiles_ref, rows_ref, window_ref, global_sum_ref,
    running_ref,
):
    place = scatter.place
    side, k, kind = index // (2 * LINE), lax.rem(index // 2, LINE), lax.rem(index, 2)
    line = scatter.order[3]
    for other in (2, 1, 0):
        line = jnp.where(k == other, scatter.order[other], line)
    x = jnp.where(side == 0, 1 - place.x, place.x)
    core = jnp.where(kind == 0, 1 - place.core, place.core)
    owner = place.at(line, x, core)
    slot = 2 * k + side
    running = None
    for pick in range(EACH):
        code = table[0, owner * EACH + pick]
        term = product(tiles_ref[code >> 6], rows_ref[(code >> 3) & 7, code & 7])
        running = term if running is None else running + term
        running_ref[pick + 1] = running
    for row in range(ROWS):
        name = owner * ROWS + row
        first = jnp.clip(table[1, name] - owner * EACH, 0, EACH)
        last = jnp.clip(table[1, name + 1] - owner * EACH, 0, EACH)
        hit = jnp.where(global_ref[0] == name, 1, 0) + jnp.where(global_ref[1] == name, 2, 0)
        near = name - place.me * ROWS + 1
        near = jnp.where((near >= 0) & (near < ROWS + 2), near, ROWS + 2)
        total = running_ref[last] - running_ref[first] + global_sum_ref[hit] + window_ref[near]
        scatter.kept[slot, row] = total * scale

    @pl.when(kind == 0)
    def _():
        scatter.pair_out[slot] = scatter.kept[slot].astype(jnp.bfloat16)
        scatter.pair(slot).start()


def fused_kernel(
    random_ref, global_ref, segment_in, query_in, grad_in, key_in, value_in,
    attended_out, query_grad_out, key_grad_out, value_grad_out,
    keys, values, key_turned, value_turned, queries, grads, flag_ref, shared_ref, picked_ref,
    dpicked_ref, inverse_ref, window_ref, global_sum_ref, running_ref, table_vec, table, segment_ref,
    attended_ref, query_grad_ref, key_grad_ref, value_grad_ref, local_sems, out_sems,
    *rest,
):
    place = Place()
    wide = jnp.float32
    total_blocks = keys.shape[0]
    key_sems, value_sems, rest = rest[:6], rest[6:12], rest[12:]
    value_scatter = Scatter(place, *rest[:13])
    key_scatter = Scatter(place, *rest[13:])
    me = place.me
    first = me * ROWS
    own = pl.ds(first, ROWS)
    loads = [
        pltpu.make_async_copy(key_in, keys.at[own], local_sems.at[0]),
        pltpu.make_async_copy(value_in, values.at[own], local_sems.at[1]),
        pltpu.make_async_copy(segment_in, segment_ref, local_sems.at[3 + 2 * HQ]),
    ]
    for head in range(HQ):
        span = pl.ds(head * HD, HD)
        loads.append(
            pltpu.make_async_copy(
                query_in.at[:, :, span], queries.at[:, head], local_sems.at[2 + head]
            )
        )
        loads.append(
            pltpu.make_async_copy(
                grad_in.at[:, :, span], grads.at[:, head], local_sems.at[2 + HQ + head]
            )
        )
    for load in loads[:3]:
        load.start()
    greet(place)
    for load in loads[:3]:
        load.wait()
    key_gather = Gather(place, keys, *key_sems)
    value_gather = Gather(place, values, *value_sems)

    def turn(source, target, owner):
        for row in range(ROWS):
            target[owner * ROWS + row] = source[owner * ROWS + row].T

    def turn_keys(owner):
        turn(keys, key_turned, owner)

    def turn_values(owner):
        turn(values, value_turned, owner)

    key_gather.start_line()
    value_gather.start_line()
    key_gather.start_cross()
    value_gather.start_cross()
    for load in loads[3:]:
        load.start()
    pick_table(random_ref, table_vec)
    table_copy = pltpu.make_async_copy(table_vec, table, local_sems.at[2 + 2 * HQ])
    table_copy.start()
    zero = jnp.zeros((BLK, HD), wide)

    def clear():
        for row in range(ROWS + 3):
            window_ref[row] = zero
        for slot in range(G + 2):
            global_sum_ref[slot] = zero

    clear()
    running_ref[0] = zero
    boundary = jnp.sum((segment_ref[...] == segment_ref[0:1, 0:1]).astype(jnp.int32))
    @pl.loop(0, total_blocks)
    def _(name):
        flag_ref[name] = key_flags(boundary, name)

    flag_ref[total_blocks] = jnp.where(
        lax.broadcasted_iota(jnp.int32, (BLK, HD), 1) < 2, 1.0, 0.0
    ).astype(jnp.bfloat16)
    key_gather.line_arrival(1)
    key_gather.cross_arrival(0)
    turn_keys(key_gather.own[0])
    turn_values(key_gather.own[0])
    key_gather.line_arrival(2)
    value_gather.cross_arrival(0)
    turn_keys(key_gather.own[1])
    turn_keys(key_gather.other[0])
    key_gather.cross_arrival(1)
    value_gather.line_arrival(1, cross=False)
    turn_values(value_gather.own[1])
    turn_values(value_gather.other[0])
    key_gather.line_arrival(3)
    value_gather.cross_late(1)
    turn_keys(key_gather.own[2])
    turn_keys(key_gather.other[1])
    value_gather.line_arrival(2)
    turn_keys(key_gather.own[3])
    turn_values(value_gather.own[2])
    key_gather.cross_arrival(2)
    turn_keys(key_gather.other[2])
    value_gather.line_arrival(3)
    turn_values(value_gather.own[3])
    for k in range(LINE - 1):
        key_gather.near_arrival(k)
        turn_keys(key_gather.own_far[k])
        key_gather.far_arrival(k)
        turn_keys(key_gather.other_far[k])
        value_gather.near_arrival(k)
        turn_values(value_gather.own_far[k])
    value_gather.far_arrival(0)
    turn_values(value_gather.other_far[0])
    key_gather.cross_arrival(3)
    key_gather.near_arrival(3)
    for load in loads[3:]:
        load.wait()
    table_copy.wait()
    key_gather.far_arrival(3)

    @pl.loop(0, ROWS)
    def _(block):
        score_block(
            block, first + block, boundary, random_ref, global_ref, queries, grads, keys,
            flag_ref, shared_ref, picked_ref, inverse_ref, window_ref, global_sum_ref,
        )
        for k in range(1, LINE):

            @pl.when(block == k - 1)
            def _(k=k):
                value_gather.cross_arrival(k)

    def owners(scatter, scale, tiles_ref, rows_ref, events):
        global_sum_ref[3] = global_sum_ref[1] + global_sum_ref[2]

        @pl.loop(0, SEQ)
        def _(index):
            sum_owner(
                index, scatter, scale, table, global_ref, tiles_ref, rows_ref, window_ref,
                global_sum_ref, running_ref,
            )
            for k in range(LINE):

                @pl.when(index == 2 * k + 6)
                def _(k=k):
                    scatter.start_cross(k)

            events(index)

    owners(value_scatter, 1.0, picked_ref, grads, lambda index: None)
    clear()
    value_gather.near_arrival(3)
    turn_values(value_gather.own_far[3])
    turn_keys(key_gather.other[3])
    turn_keys(key_gather.own_far[3])
    turn_keys(key_gather.other_far[3])
    for k in range(1, LINE):
        turn_values(value_gather.other[k])
        value_gather.far_arrival(k)
        turn_values(value_gather.other_far[k])
    edge, inner = place.inner == 0, place.inner == 1

    def block_out(block):
        return [
            pltpu.make_async_copy(source.at[block], target.at[block], out_sems.at[at * ROWS + block])
            for at, (source, target) in enumerate(
                [(attended_ref, attended_out), (query_grad_ref, query_grad_out)]
            )
        ]

    value_out = pltpu.make_async_copy(value_grad_ref, value_grad_out, out_sems.at[2 * ROWS])
    key_out = pltpu.make_async_copy(key_grad_ref, key_grad_out, out_sems.at[2 * ROWS + 1])

    @pl.loop(0, ROWS)
    def _(block):
        grad_block(
            block, first + block, random_ref, global_ref, queries, grads, values, key_turned,
            value_turned, shared_ref, picked_ref, dpicked_ref, inverse_ref, window_ref,
            global_sum_ref, attended_ref, query_grad_ref,
        )
        for copy in block_out(block):
            copy.start()
        for k in range(3):

            @pl.when((block == k + 1) & edge)
            def _(k=k):
                value_scatter.edge_hop(k)

        @pl.when((block == 3) & inner)
        def _():
            value_scatter.inner_hop(0)

    def between(index):
        for k in (1, 2):

            @pl.when((index == 4 * k + 7) & inner)
            def _(k=k):
                value_scatter.inner_hop(k)

    owners(key_scatter, 1.0 / math.sqrt(HD), dpicked_ref, queries, between)

    @pl.when(edge)
    def _():
        key_scatter.edge_hop(0)
        key_scatter.edge_hop(1)
        value_scatter.edge_finish(value_grad_ref)
        key_scatter.edge_hop(2)
        key_scatter.edge_finish(key_grad_ref)

    @pl.when(inner)
    def _():
        value_scatter.inner_finish(value_grad_ref)
        for k in range(LINE - 1):
            key_scatter.inner_hop(k)
        key_scatter.inner_finish(key_grad_ref)

    value_out.start()
    key_out.start()
    key_gather.wait_sends()
    value_gather.wait_sends()
    value_scatter.wait_sends()
    key_scatter.wait_sends()
    for block in range(ROWS):
        for copy in block_out(block):
            copy.wait()
    value_out.wait()
    key_out.wait()


def deliver_kernel(*refs):
    count = (len(refs) - 1) // 3
    sources, targets, held, sems = refs[:count], refs[count : 2 * count], refs[2 * count : -1], refs[-1]
    loads = [
        pltpu.make_async_copy(sources[i], held[i], sems.at[i]) for i in range(count)
    ]
    stores = [
        pltpu.make_async_copy(held[i], targets[i], sems.at[count + i]) for i in range(count)
    ]
    for load in loads:
        load.start()
    for load, store in zip(loads, stores):
        load.wait()
        store.start()
    for store in stores:
        store.wait()


def deliver(*arrays):
    count = len(arrays)
    return pl.pallas_call(
        deliver_kernel,
        in_specs=[pl.BlockSpec(memory_space=pltpu.HBM)] * count,
        out_specs=[pl.BlockSpec(memory_space=pltpu.HBM)] * count,
        out_shape=[jax.ShapeDtypeStruct(a.shape, a.dtype) for a in arrays],
        scratch_shapes=[pltpu.VMEM(a.shape, a.dtype) for a in arrays]
        + [pltpu.SemaphoreType.DMA((2 * count,))],
        compiler_params=pltpu.CompilerParams(vmem_limit_bytes=FUSED_MIB * 1024 * 1024),
        name="deliver",
    )(*arrays)


def fused_call(random_ids, global_ids, segments, queries, out_grads, keys, values):
    smem = pl.BlockSpec(memory_space=pltpu.SMEM)
    hbm = pl.BlockSpec(memory_space=pltpu.HBM)
    half = jnp.bfloat16
    wide = jnp.float32
    total_blocks = SEQ * ROWS
    dma = pltpu.SemaphoreType.DMA

    def tiles(*count, kind=half):
        return pltpu.VMEM(count + (BLK, HD), kind)

    gather_sems = [
        dma((count * HALVES,)) for count in (5, LINE, LINE, LINE, 2 * LINE, 2 * LINE)
    ]
    scatter_parts = [
        tiles(2 * LINE, ROWS, kind=wide),
        tiles(2 * LINE, ROWS),
        tiles(2 * LINE, ROWS),
        tiles(LINE, ROWS),
        tiles(LINE, ROWS),
        tiles(LINE - 1, ROWS),
        tiles(5, ROWS),
    ] + [dma((count,)) for count in (2 * LINE, 2 * LINE, LINE * HALVES, LINE * HALVES, 3 * HALVES, 5 * HALVES)]
    return pl.pallas_call(
        fused_kernel,
        in_specs=[smem, smem, hbm, hbm, hbm, hbm, hbm],
        out_specs=[hbm] * 4,
        out_shape=[
            jax.ShapeDtypeStruct((ROWS, BLK, HQ * HD), half),
            jax.ShapeDtypeStruct((ROWS, BLK, HQ * HD), half),
            jax.ShapeDtypeStruct(keys.shape, half),
            jax.ShapeDtypeStruct(keys.shape, half),
        ],
        scratch_shapes=[
            tiles(total_blocks),
            tiles(total_blocks),
            tiles(total_blocks),
            tiles(total_blocks),
            tiles(ROWS, HQ),
            tiles(ROWS, HQ),
            tiles(total_blocks + 1),
            pltpu.VMEM((ROWS, 5, BLK, HQ * BLK), half),
            tiles(PICKS),
            tiles(PICKS),
            pltpu.VMEM((ROWS, 8, HQ * BLK), wide),
            tiles(ROWS + 3, kind=wide),
            tiles(G + 2, kind=wide),
            tiles(EACH + 1, kind=wide),
            pltpu.VMEM((8, BLK), jnp.int32),
            pltpu.SMEM((8, BLK), jnp.int32),
            pltpu.VMEM((total_blocks, BLK), jnp.int32),
            pltpu.VMEM((ROWS, BLK, HQ * HD), half),
            pltpu.VMEM((ROWS, BLK, HQ * HD), half),
            tiles(ROWS),
            tiles(ROWS),
            dma((4 + 2 * HQ,)),
            dma((2 * ROWS + 2,)),
        ]
        + gather_sems * 2
        + scatter_parts * 2,
        compiler_params=pltpu.CompilerParams(
            collective_id=0, has_side_effects=True, vmem_limit_bytes=FUSED_MIB * 1024 * 1024
        ),
        name="fused_attention",
    )(random_ids, global_ids, segments, queries, out_grads, keys, values)


FUSED_MIB = 60


def fused_body(queries, key_rows, value_rows, out_grads, segment_ids, random_blocks, global_blocks):
    total_blocks = segment_ids.shape[0] // BLK

    def blocks(array):
        return array.reshape(ROWS, BLK, -1)

    attended, query_grads, key_grads, value_grads = fused_call(
        random_blocks.transpose(2, 0, 1),
        global_blocks,
        segment_ids.reshape(total_blocks, BLK),
        blocks(queries),
        blocks(out_grads),
        blocks(key_rows),
        blocks(value_rows),
    )
    tokens = ROWS * BLK
    return deliver(
        attended.reshape(tokens, -1),
        query_grads.reshape(tokens, -1),
        key_grads.reshape(tokens, -1),
        value_grads.reshape(tokens, -1),
    )


def plan(*arrays):
    tokens = arrays[4].shape[0]
    fits = tokens * 2 * HD * 4 <= DENSE_BYTES
    chosen = fused_body if fits and arrays[0].shape[0] == ROWS * BLK and lax.axis_size("seq") == SEQ else body
    return chosen(*arrays)


def solution(mesh):
    placed = (
        P(("shard", "seq"), None),
        P(("shard", "seq"), None),
        P(("shard", "seq"), None),
        P(("shard", "seq"), None),
        P("shard"),
        P(("shard", "seq"), None, None),
        P("shard"),
    )
    return jax.shard_map(
        plan,
        mesh=mesh,
        in_specs=placed,
        out_specs=(
            P(("shard", "seq"), None),
            P(("shard", "seq"), None),
            P(("shard", "seq"), None),
            P(("shard", "seq"), None),
        ),
        check_vma=False,
    )
```
